32 devices in a mesh: snp: 8 (over y, x, core), samp: 4 (over z).
Axes of the slice: x: 2, y: 2, z: 4, core: 2. Of those that a mesh axis runs over, the one named last changes fastest.
Arguments:
- genotypes: bfloat16 [2048, 2, 1024], P('samp', None, 'snp'), may hold values from 0.06 to 0.79, as said below
- case_labels: int32 [2048], P('samp'), may hold values from 0 to 1, as said below
- refit_own: int32 [128], P('snp'), may hold values from 0 to 127
- refit_peer: int32 [128], P('snp'), may hold values from 0 to 1023, as said below
Outputs:
- screen: float32 [1024, 4, 128], P(('snp', 'samp'))
- refit_stat: float32 [128], P('snp')
The draws below stay inside these ranges and needn't reach their ends.
Inputs may be any that keep to these rules, and one draw needn't show every extreme that they name: `genotypes`: each entry is at least 0.06, and the two probabilities of a sample and SNP sum to at most 0.94. `case_labels`: both classes occur. `refit_peer`: within each aligned block of 16 entries (the pairs of one SNP block), at most 4 entries name SNPs of any one block of 128 SNPs, and some block is named exactly 4 times.
All inputs are finite; a program needn't handle non-finite values.
Results may differ from the reference program's by a relative error of at most 0.0035.
Values may be sent and summed in bfloat16 or wider, within the bound.
No kernel may reach another device: no remote copies, remote signals or barrier semaphores. Data moves between devices by JAX's collectives and lax.ppermute only.
A program may use at most 64 MiB of HBM per device.

```python
import jax
import jax.numpy as jnp
from jax import lax

BLK = 128
HALF = 2
CAP = 4
LIST = 16
ITERS = 10
SNPS = 1024
SAMPLES = 2048
PAIRS = 128
N_SNP = 8


def shared_labels(key):
    raw_labels = jax.random.randint(jax.random.fold_in(key, 11), (SAMPLES,), 0, 2)
    position = jnp.arange(SAMPLES)
    raw_labels = jnp.where(position == 0, 1, raw_labels)
    raw_labels = jnp.where(position == SAMPLES - 1, 0, raw_labels)
    return raw_labels.astype(jnp.int32)


def draw_case_labels(key, part):
    return shared_labels(key)


def draw_genotypes(key, part):
    labels_wide = shared_labels(key).astype(jnp.float32)
    subkeys = jax.random.split(jax.random.fold_in(key, 23), 4)
    latent = 1.2 * (labels_wide - 0.5) + jax.random.normal(subkeys[0], (SAMPLES,))
    baseline = jax.random.uniform(subkeys[1], (3, SNPS), minval=-0.5, maxval=0.5)
    slopes = jax.random.uniform(subkeys[2], (SNPS,), minval=0.2, maxval=0.9)
    jitter = jax.random.uniform(subkeys[3], (SAMPLES, 3, SNPS), minval=-0.7, maxval=0.7)
    copies = jnp.array([-1.0, 0.0, 1.0], dtype=jnp.float32)
    logits = jnp.tanh(baseline[None] + slopes[None, None, :] * copies[None, :, None] * latent[:, None, None] + jitter)
    probability = jax.nn.softmax(logits, axis=1)
    return probability[:, :2, :].astype(jnp.bfloat16)


def draw_refit_peer(key, part):
    blocks = SNPS // BLK

    def one_block(block_key):
        subkeys = jax.random.split(block_key, 5)
        heat = jax.random.randint(subkeys[0], (blocks,), 0, 3)
        favored = jax.random.randint(subkeys[1], (), 0, blocks)
        heat = jnp.where(jnp.arange(blocks) == favored, 3, heat)
        slot_heat = jnp.repeat(heat, CAP)
        jitter = jax.random.randint(subkeys[2], (blocks * CAP,), 0, 2 ** 19)
        scores = (jitter + slot_heat * 2 ** 19) * (blocks * CAP) + jnp.arange(blocks * CAP)
        picked_scores, chosen = lax.top_k(scores.astype(jnp.int32), LIST)
        peer_block = chosen // CAP
        shuffle = jax.random.permutation(subkeys[3], LIST)
        peer_block = peer_block[shuffle]
        local = jax.random.randint(subkeys[4], (LIST,), 0, BLK)
        return (peer_block * BLK + local).astype(jnp.int32)
    block_keys = jax.random.split(key, blocks)
    return jax.vmap(one_block)(block_keys).reshape(-1)


def place_ends(values, own_key, low, top_value):
    shape = values.shape
    place = [jax.random.randint(jax.random.fold_in(own_key, axis), (), 0, shape[axis]) for axis in range(len(shape))]
    values = values.at[tuple(place)].set(low)
    longest = shape.index(max(shape))
    place[longest] = (place[longest] + 1) % shape[longest]
    return values.at[tuple(place)].set(top_value)


def setup_inputs(seed: int = 0) -> dict:
    streams_of = jax.random.split(jax.random.key(seed), 5)
    genotypes = draw_genotypes(jax.random.fold_in(streams_of[4], 71), 0)
    case_labels = draw_case_labels(jax.random.fold_in(streams_of[4], 71), 0)
    refit_own = place_ends(jax.random.randint(streams_of[2], (PAIRS,), 0, BLK), jax.random.fold_in(streams_of[2], 1), 0, BLK - 1).astype(jnp.int32)
    refit_peer = draw_refit_peer(jax.random.fold_in(streams_of[4], 71), 0)
    return dict(genotypes=genotypes, case_labels=case_labels, refit_own=refit_own, refit_peer=refit_peer)


def complete(inner_cells, margin_a, margin_b, totals):
    target = inner_cells.shape[:2] + inner_cells.shape[3:]
    margin_a = jnp.broadcast_to(margin_a, target)
    margin_b = jnp.broadcast_to(margin_b, target)
    third_col = margin_a - inner_cells[:, :, 0] - inner_cells[:, :, 1]
    third_row = margin_b - inner_cells[:, 0] - inner_cells[:, 1]
    corner = totals - margin_a[:, 0] - margin_a[:, 1] - third_row[:, 0] - third_row[:, 1]
    top_rows = jnp.concatenate([inner_cells, third_col[:, :, None]], axis=2)
    last_row = jnp.concatenate([third_row, corner[:, None]], axis=1)
    return jnp.concatenate([top_rows, last_row[:, None]], axis=1)


def kirkwood(table):
    pair_sum = jnp.sum(table, axis=0)
    class_a = jnp.sum(table, axis=2)
    class_b = jnp.sum(table, axis=1)
    single_a = jnp.sum(pair_sum, axis=1)
    single_b = jnp.sum(pair_sum, axis=0)
    class_sum = jnp.sum(class_a, axis=1)
    grand_total = jnp.sum(class_sum, axis=0)
    approx = pair_sum[None] * class_a[:, :, None] * class_b[:, None, :] / (
        single_a[None, :, None] * single_b[None, None, :] * class_sum[:, None, None])
    scale_sum = jnp.sum(approx, axis=(0, 1, 2))
    return 2.0 * jnp.sum(table * jnp.log(table * scale_sum / (grand_total * approx)), axis=(0, 1, 2))


def refit(table):
    def sweep(number, fitted):
        fitted = fitted * (jnp.sum(table, axis=0) / jnp.sum(fitted, axis=0))[None]
        fitted = fitted * (jnp.sum(table, axis=2) / jnp.sum(fitted, axis=2))[:, :, None]
        fitted = fitted * (jnp.sum(table, axis=1) / jnp.sum(fitted, axis=1))[:, None]
        return fitted
    fitted = lax.fori_loop(0, ITERS, sweep, jnp.ones_like(table))
    return 2.0 * jnp.sum(table * jnp.log(table / fitted), axis=(0, 1, 2))


def tile_cells(owner, visitor, classes):
    samples = owner.shape[0]
    block = owner.shape[2]
    weighted = (visitor[:, None] * classes[:, :, None, None]).reshape(samples, 4 * block)
    product = lax.dot_general(owner.reshape(samples, 2 * block), weighted,
                              (((0,), (0,)), ((), ())), preferred_element_type=jnp.float32)
    return product.reshape(2, block, 2, 2, block)


def reference(genotypes, case_labels, refit_own, refit_peer):
    samples = genotypes.shape[0]
    weight = case_labels.astype(jnp.float32)
    classes = jnp.stack([weight, 1.0 - weight], axis=1).astype(jnp.bfloat16)
    margin = jnp.dot(classes.T, genotypes.reshape(samples, 2 * SNPS),
                     preferred_element_type=jnp.float32).reshape(2, 2, SNPS)
    counts = jnp.sum(classes.astype(jnp.float32), axis=0)
    offsets = list(range(-1, -HALF - 1, -1)) + list(range(1, HALF + 1))

    def screen_block(block_index):
        first_row = (block_index * BLK).astype(jnp.int32)
        owner = lax.dynamic_slice_in_dim(genotypes, first_row, BLK, 2)
        margin_a = lax.dynamic_slice_in_dim(margin, first_row, BLK, 2)[:, :, :, None]
        results = []
        for offset in offsets:
            other_start = ((block_index + offset) % N_SNP * BLK).astype(jnp.int32)
            visitor = lax.dynamic_slice_in_dim(genotypes, other_start, BLK, 2)
            inner_cells = tile_cells(owner, visitor, classes).transpose(2, 0, 3, 1, 4)
            margin_b = lax.dynamic_slice_in_dim(margin, other_start, BLK, 2)[:, :, None, :]
            results.append(kirkwood(complete(inner_cells, margin_a, margin_b, counts[:, None, None])))
        return jnp.stack(results, axis=1)

    screen = lax.map(screen_block, jnp.arange(N_SNP, dtype=jnp.int32)).reshape(SNPS, 2 * HALF, BLK)

    own_groups = refit_own.reshape(N_SNP, LIST)
    peer_groups = refit_peer.reshape(N_SNP, LIST)
    classes_wide = classes.astype(jnp.float32)

    def refit_block(inputs):
        block_index, own_local, peer_global = inputs
        own_global = (block_index * BLK + own_local).astype(jnp.int32)
        first_cols = jnp.take(genotypes, own_global, axis=2).astype(jnp.float32)
        second_cols = jnp.take(genotypes, peer_global, axis=2).astype(jnp.float32)
        product = first_cols[:, :, None, :] * second_cols[:, None, :, :]
        inner_cells = jnp.einsum('sijr,sc->cijr', product, classes_wide, precision=lax.Precision.HIGHEST)
        table = complete(inner_cells, margin[:, :, own_global], margin[:, :, peer_global], counts[:, None])
        return refit(table)

    refit_stat = lax.map(refit_block, (jnp.arange(N_SNP, dtype=jnp.int32), own_groups, peer_groups)).reshape(PAIRS)
    return screen, refit_stat
```

```python
import functools

import jax
import jax.numpy as jnp
from jax import lax
from jax.experimental import pallas as pl
from jax.experimental.pallas import tpu as pltpu
from jax.sharding import PartitionSpec as P

HALF = 2
CAP = 4
ITERS = 10
MIDDLE = 0.47
SPREAD = 0.411
F32 = jnp.float32
BF16 = jnp.bfloat16


def iota(shape, axis):
    return lax.broadcasted_iota(jnp.int32, shape, axis)


def by_t(a, b):
    return lax.dot_general(a, b, (((1,), (1,)), ((), ())), preferred_element_type=F32)


def dot(a, b):
    return lax.dot_general(a, b, (((1,), (0,)), ((), ())), preferred_element_type=F32)


def earlier(count):
    return (iota((count, count), 0) < iota((count, count), 1)).astype(BF16)


def split_genotypes(ref, wide):
    rows = wide.shape[0]
    wide[...] = ref[0:rows, :].astype(F32)
    return [wide[pl.ds(j, rows // 2, stride=2), :] for j in range(2)]


def select_kernel(ids, geno, sent, wide, *, shift):
    here = lax.axis_index("snp")
    blocks, pairs = ids.shape
    block = geno.shape[1]
    rows = blocks * 2 * CAP
    names = ids[...]
    local = (names & (block - 1)).astype(F32)
    hit = (lax.shift_right_logical(names, shift) == here).astype(F32)
    rank = dot(hit.astype(BF16), earlier(pairs))
    spread = (lax.shift_right_logical(iota((rows, blocks), 0), 3) == iota((rows, blocks), 1)).astype(BF16)
    hit_rows = dot(spread, hit.astype(BF16))
    rank_rows = dot(spread, rank.astype(BF16))
    local_rows = dot(spread, local.astype(BF16))
    slot = (iota((rows, pairs), 0) & (CAP - 1)).astype(F32)
    chosen = jnp.where(rank_rows == slot, hit_rows, 0.0)
    column = jnp.sum(chosen * local_rows, axis=1, keepdims=True)
    valid = jnp.sum(chosen, axis=1, keepdims=True)
    which = iota((rows, block), 1).astype(F32)
    second = (iota((rows, block), 0) & CAP) > 0
    one_hot = jnp.where((which == column) & (valid > 0.5), 1.0, 0.0)
    low = jnp.where(second, 0.0, one_hot).astype(BF16)
    high = jnp.where(second, one_hot, 0.0).astype(BF16)
    g0, g1 = split_genotypes(geno, wide)
    sent[...] = (by_t(low, g0.astype(BF16)) + by_t(high, g1.astype(BF16))).astype(BF16)


def fixed(value, samples):
    return (value * 2.0 ** (30 - (samples - 1).bit_length())).astype(jnp.int32)


def floating(value, samples):
    return value.astype(F32) * 2.0 ** ((samples - 1).bit_length() - 30)


def code_step(count):
    return jnp.maximum(count, 1.0) * (SPREAD * SPREAD / 32767.0)


def quantized(value, step):
    scaled = value * (1.0 / step)
    return jnp.clip(jnp.floor(scaled + 0.5), -32767.0, 32767.0).astype(jnp.int32)


def class_rows(label0, tail):
    case0 = label0[...].astype(F32)
    case1 = jnp.concatenate([tail[q:q + 1, :].astype(F32) for q in range(case0.shape[1] // tail.shape[1])], axis=1)
    case = jnp.concatenate([case0, case1], axis=1)
    return [case, 1.0 - case]


def coded_tiles(first_refs, second_refs, classes, left, right, wide, outs):
    k = lax.axis_index("samp")
    samples = wide.shape[0] // 2
    block = wide.shape[1]
    quarter = block // 4
    first_slab = None
    for half in range(2):
        rows = pl.ds(half * samples, samples)
        parts = split_genotypes(first_refs[half], wide)
        if half == 0:
            first_slab = [p.astype(BF16) for p in parts]
        for i in range(2):
            turned = parts[i].T
            for c in range(2):
                piece = (turned * classes[c][:, half * samples:(half + 1) * samples]).astype(BF16)
                for q in range(4):
                    d = (q + 4 - k) & 3
                    left[d, c * 2 + i, :, rows] = piece[q * quarter:(q + 1) * quarter]
        parts = split_genotypes(second_refs[half], wide)
        for j in range(2):
            right[rows, j * block:(j + 1) * block] = parts[j].astype(BF16)
    lhs = left[...].reshape(16 * quarter, 2 * samples)
    cells = dot(lhs, right[...])
    row_sums = dot(lhs, jnp.ones((2 * samples, block), BF16))
    weights = jnp.concatenate(classes + [jnp.zeros((6, 2 * samples), F32)], axis=0).astype(BF16)
    column_sums = dot(weights, right[...])
    lanes = jnp.ones((1, 2 * block), F32)
    counts = [jnp.sum(classes[c], axis=1, keepdims=True) * lanes for c in range(2)]
    for d in range(4):
        words = None
        for c in range(2):
            rows = slice((d * 2 + c) * 2 * quarter, (d * 2 + c + 1) * 2 * quarter)
            row = row_sums[rows]
            base = jnp.concatenate([row, row], axis=1)
            centred = cells[rows] - MIDDLE * (base + column_sums[c:c + 1]) + (MIDDLE * MIDDLE) * counts[c]
            code = quantized(centred, code_step(counts[c]))
            words = lax.shift_left(code, 16) if c == 0 else words | (code & 0xFFFF)
        outs[d][0:2 * quarter, :] = words
    return first_slab, column_sums, counts


def write_tails(outs, start, samples, columns, own, counts):
    parts = [fixed(v, 2 * samples) for v in (columns[0:2], own[0:2], counts[0], counts[1])]
    tail = jnp.concatenate(parts + [jnp.zeros((2, columns.shape[1]), jnp.int32)], axis=0)
    for out in outs:
        out[start:start + 8, :] = tail


def ahead_kernel(own0, own1, other0, other1, label0, a0, a1, a2, a3, sums, wide, left, right):
    samples = wide.shape[0] // 2
    classes = class_rows(label0, own1[2 * samples:, :])
    outs = (a0, a1, a2, a3)
    _, columns, counts = coded_tiles((other0, other1), (own0, own1), classes, left, right, wide, outs)
    write_tails(outs, wide.shape[1] // 2, samples, columns, columns, counts)
    sums[...] = columns


def behind_kernel(own0, own1, other0, other1, label0, own_ids, peer_ids, got, sums,
                  b0, b1, b2, b3, wide, left, right, *, shift):
    samples = wide.shape[0] // 2
    block = wide.shape[1]
    classes = class_rows(label0, own1[2 * samples:, :])
    outs = (b0, b1, b2, b3)
    own_slab, columns, counts = coded_tiles((own0, own1), (other0, other1), classes, left, right, wide, outs)
    write_tails(outs, block // 2, samples, columns, sums[...], counts)

    pairs = peer_ids.shape[1]
    rows = got.shape[0]
    blocks = rows // (2 * CAP)
    peers = lax.shift_right_logical(peer_ids[...], shift)
    member = (iota((blocks, pairs), 0) == peers).astype(F32)
    before = dot(member.astype(BF16), earlier(pairs))
    rank = jnp.sum(member * before, axis=0, keepdims=True)
    row = iota((rows, pairs), 0)
    row_block = lax.shift_right_logical(row, 3)
    row_slot = (row & (2 * CAP - 1)).astype(F32)
    first_pick = (iota((block, pairs), 0) == own_ids[...]).astype(F32).T.astype(BF16)
    first, second = [], []
    for j in range(2):
        pick = jnp.where((row_block == peers) & (row_slot == rank + float(CAP * j)), 1.0, 0.0).T.astype(BF16)
        second.append(dot(pick, got[...]))
        first.append(by_t(first_pick, own_slab[j]))
    slab = [classes[c][:, 0:samples] for c in range(2)]
    values = []
    for c in range(2):
        for i in range(2):
            mine = first[i] * slab[c]
            for j in range(2):
                values.append(jnp.sum(mine * second[j], axis=1, keepdims=True))
    for side in (first, second):
        for c in range(2):
            for i in range(2):
                values.append(jnp.sum(side[i] * slab[c], axis=1, keepdims=True))
    lane = iota((pairs, 2 * block), 1)
    refit = jnp.zeros((pairs, 2 * block), F32)
    for v, value in enumerate(values):
        refit = jnp.where(lane == v, value, refit)
    refit = fixed(refit, 2 * samples)
    for out in outs:
        out[block // 2 + 8:, :] = refit


def complete(cells, margin_a, margin_b, totals):
    table = [[[None] * 3 for _ in range(3)] for _ in range(2)]
    for c in range(2):
        n = table[c]
        for i in range(2):
            for j in range(2):
                n[i][j] = cells[c][i][j]
            n[i][2] = margin_a[c][i] - n[i][0] - n[i][1]
        for j in range(2):
            n[2][j] = margin_b[c][j] - n[0][j] - n[1][j]
        n[2][2] = (totals[c] - margin_a[c][0] - margin_a[c][1]) - n[2][0] - n[2][1]
    return table


def kirkwood(n, margin_a, margin_b, totals):
    row_ic = [[margin_a[c][0], margin_a[c][1], totals[c] - margin_a[c][0] - margin_a[c][1]] for c in range(2)]
    col_jc = [[margin_b[c][0], margin_b[c][1], totals[c] - margin_b[c][0] - margin_b[c][1]] for c in range(2)]
    single_a = [row_ic[0][i] + row_ic[1][i] for i in range(3)]
    single_b = [col_jc[0][j] + col_jc[1][j] for j in range(3)]
    grand = totals[0] + totals[1]
    inv_a = [1.0 / s for s in single_a]
    row_x = [[row_ic[c][i] * inv_a[i] / totals[c] for i in range(3)] for c in range(2)]
    col_y = [[col_jc[c][j] / single_b[j] for j in range(3)] for c in range(2)]
    scale = None
    approx = {}
    for i in range(3):
        for j in range(3):
            pair = n[0][i][j] + n[1][i][j]
            for c in range(2):
                value = pair * row_x[c][i] * col_y[c][j]
                approx[c, i, j] = value
                scale = value if scale is None else scale + value
    factor = scale / grand
    total = None
    for (c, i, j), value in approx.items():
        term = n[c][i][j] * jnp.log(n[c][i][j] * factor / value)
        total = term if total is None else total + term
    return 2.0 * total


def finish_kernel(b0, b1, b2, b3, a0, a1, a2, a3, screen, stat, columns, *, samples):
    k = lax.axis_index("samp")
    bs, as_ = (b0, b1, b2, b3), (a0, a1, a2, a3)
    block = b0.shape[1] // 2
    quarter = block // 4
    height = 2 * quarter
    pairs = stat.shape[1]

    def both(x, y, row, lanes=slice(0, block)):
        return floating(x[row:row + 1, lanes], 2 * samples) + floating(y[row:row + 1, lanes], 2 * samples)

    lanes_of = [slice(j * block, (j + 1) * block) for j in range(2)]
    totals_row = [both(b0, b2, height + 4 + c) for c in range(2)]
    own = [both(b0, b2, height + 2 + c, lanes_of[i]) for c in range(2) for i in range(2)]
    columns[...] = jnp.concatenate(own + [jnp.zeros((block - 4, block), F32)], axis=0).T
    mine = columns[pl.ds(pl.multiple_of(k * quarter, quarter), quarter), :]
    margin_a = [[jnp.broadcast_to(mine[:, c * 2 + i:c * 2 + i + 1], (quarter, block)) for i in range(2)] for c in range(2)]

    stats = []
    for msgs in (bs, as_):
        for parity in range(2):
            x, y = msgs[parity], msgs[parity + 2]
            steps = [[code_step(floating(m[height + 4 + c:height + 5 + c, 0:block], 2 * samples)) for m in (x, y)]
                     for c in range(2)]
            margin_b = [[both(x, y, height + c, lanes_of[j]) for j in range(2)] for c in range(2)]
            cells = [[[None, None], [None, None]] for _ in range(2)]
            for i in range(2):
                for j in range(2):
                    words = [m[i * quarter:(i + 1) * quarter, lanes_of[j]] for m in (x, y)]
                    for c in range(2):
                        codes = [lax.shift_right_arithmetic(w if c == 0 else lax.shift_left(w, 16), 16) for w in words]
                        base = MIDDLE * (margin_a[c][i] + margin_b[c][j]) - (MIDDLE * MIDDLE) * totals_row[c]
                        cells[c][i][j] = (codes[0].astype(F32) * steps[c][0] + codes[1].astype(F32) * steps[c][1]) + base
            table = complete(cells, margin_a, margin_b, totals_row)
            stats.append(kirkwood(table, margin_a, margin_b, totals_row))
    even = (k & 1) == 0
    for side in range(2):
        e, o = stats[2 * side], stats[2 * side + 1]
        screen[:, 2 * side, :] = jnp.where(even, e, o)
        screen[:, 2 * side + 1, :] = jnp.where(even, o, e)

    for start in range(0, pairs, block):
        count = min(block, pairs - start)
        rows = slice(height + 8 + start, height + 8 + start + count)
        sums = sum(floating(m[rows, 0:block], 2 * samples) for m in bs[1:]) + floating(b0[rows, 0:block], 2 * samples)
        if count < block:
            sums = jnp.concatenate([sums, jnp.ones((block - count, block), F32)], axis=0)
        turned = sums.T
        row = [turned[v:v + 1, :] for v in range(16)]
        cells = [[[row[c * 4 + i * 2 + j] for j in range(2)] for i in range(2)] for c in range(2)]
        ma = [[row[8 + c * 2 + i] for i in range(2)] for c in range(2)]
        mb = [[row[12 + c * 2 + j] for j in range(2)] for c in range(2)]
        n = complete(cells, ma, mb, totals_row)
        n_ij = [[n[0][i][j] + n[1][i][j] for j in range(3)] for i in range(3)]
        n_ic = [[n[c][i][0] + n[c][i][1] + n[c][i][2] for i in range(3)] for c in range(2)]
        n_jc = [[n[c][0][j] + n[c][1][j] + n[c][2][j] for j in range(3)] for c in range(2)]

        def sweep(_, flat):
            f = [[[flat[c * 9 + i * 3 + j] for j in range(3)] for i in range(3)] for c in range(2)]
            for i in range(3):
                for j in range(3):
                    ratio = n_ij[i][j] / (f[0][i][j] + f[1][i][j])
                    for c in range(2):
                        f[c][i][j] = f[c][i][j] * ratio
            for c in range(2):
                for i in range(3):
                    ratio = n_ic[c][i] / (f[c][i][0] + f[c][i][1] + f[c][i][2])
                    for j in range(3):
                        f[c][i][j] = f[c][i][j] * ratio
                for j in range(3):
                    ratio = n_jc[c][j] / (f[c][0][j] + f[c][1][j] + f[c][2][j])
                    for i in range(3):
                        f[c][i][j] = f[c][i][j] * ratio
            return tuple(f[c][i][j] for c in range(2) for i in range(3) for j in range(3))

        fitted = lax.fori_loop(0, ITERS, sweep, tuple(jnp.ones((1, block), F32) for _ in range(18)))
        total = None
        for c in range(2):
            for i in range(3):
                for j in range(3):
                    term = n[c][i][j] * jnp.log(n[c][i][j] / fitted[c * 9 + i * 3 + j])
                    total = term if total is None else total + term
        stat[:, start:start + count] = (2.0 * total)[:, 0:count]


def vmem(count):
    return [pl.BlockSpec(memory_space=pltpu.VMEM)] * count


def run(body, args, outs, scratch):
    return pl.pallas_call(
        body,
        out_shape=outs,
        in_specs=vmem(len(args)),
        out_specs=jax.tree.map(lambda _: pl.BlockSpec(memory_space=pltpu.VMEM), outs),
        scratch_shapes=scratch,
    )(*args)


def on_device(genotypes, case_labels, refit_own, refit_peer):
    samples, _, block = genotypes.shape
    pairs = refit_peer.shape[0]
    snp_count = lax.axis_size("snp")
    samp_count = lax.axis_size("samp")
    assert samp_count == 2 * HALF and block & (block - 1) == 0
    shift = block.bit_length() - 1
    here = lax.axis_index("snp")

    def moved(value, where):
        links = []
        for b in range(snp_count):
            for k in range(samp_count):
                to_b, to_k = where(b, k)
                links.append((b * samp_count + k, (to_b % snp_count) * samp_count + to_k % samp_count))
        return lax.ppermute(value, ("snp", "samp"), links)

    geno = genotypes.reshape(2 * samples, block)
    labels = case_labels.reshape(1, samples)
    marks = jnp.pad(case_labels.astype(BF16).reshape(samples // block, block), ((0, -(samples // block) % 8), (0, 0)))
    other0 = moved(geno, lambda b, k: (b + 1 + (k & 1), k))
    other1 = moved(geno, lambda b, k: (b + 2 - (k & 1), k ^ 1))
    own1 = moved(jnp.concatenate([geno, marks], axis=0), lambda b, k: (b, k ^ 1))
    ids = lax.psum(jnp.where(iota((snp_count, pairs), 0) == here, refit_peer[None, :], 0), "snp")
    wide = pltpu.VMEM((2 * samples, block), F32)
    sent = run(
        functools.partial(select_kernel, shift=shift), (ids, geno),
        jax.ShapeDtypeStruct((snp_count * 2 * CAP, samples), BF16), [wide],
    )
    got = lax.all_to_all(sent, "snp", split_axis=0, concat_axis=0, tiled=True)
    scratch = [wide, pltpu.VMEM((4, 4, block // 4, 2 * samples), BF16), pltpu.VMEM((2 * samples, 2 * block), BF16)]
    short = jax.ShapeDtypeStruct((block // 2 + 8, 2 * block), jnp.int32)
    tall = jax.ShapeDtypeStruct((block // 2 + 8 + pairs, 2 * block), jnp.int32)
    *ahead, sums = run(
        ahead_kernel, (geno, own1, other0, other1, labels),
        [short] * 4 + [jax.ShapeDtypeStruct((8, 2 * block), F32)], scratch,
    )
    for d in range(4):
        ahead[d] = moved(ahead[d], lambda b, k: (b - 1 - (k & 1), k + d))
    behind = run(
        functools.partial(behind_kernel, shift=shift),
        (geno, own1, other0, other1, labels, refit_own[None, :], refit_peer[None, :], got, sums),
        [tall] * 4, scratch,
    )
    behind = list(behind)
    for d in range(1, 4):
        behind[d] = moved(behind[d], lambda b, k: (b, k + d))
    screen, stat = run(
        functools.partial(finish_kernel, samples=samples), (*behind, *ahead),
        [jax.ShapeDtypeStruct((block // samp_count, 2 * HALF, block), F32), jax.ShapeDtypeStruct((1, pairs), F32)],
        [pltpu.VMEM((block, block), F32)],
    )
    return screen, stat.reshape(pairs)


def solution(mesh):
    in_specs = (P("samp", None, "snp"), P("samp"), P("snp"), P("snp"))
    out_specs = (P(("snp", "samp"), None, None), P("snp"))
    return jax.shard_map(on_device, mesh=mesh, in_specs=in_specs, out_specs=out_specs, check_vma=False)
```

```python
import functools

import jax
import jax.numpy as jnp
from jax import lax
from jax.experimental import pallas as pl
from jax.experimental.pallas import tpu as pltpu
from jax.sharding import PartitionSpec as P

HALF = 2
CAP = 4
ITERS = 10
MIDDLE = 0.47
SPREAD = 0.411
F32 = jnp.float32
BF16 = jnp.bfloat16


def iota(shape, axis):
    return lax.broadcasted_iota(jnp.int32, shape, axis)


def by_t(a, b):
    return lax.dot_general(a, b, (((1,), (1,)), ((), ())), preferred_element_type=F32)


def dot(a, b):
    return lax.dot_general(a, b, (((1,), (0,)), ((), ())), preferred_element_type=F32)


def earlier(count):
    return (iota((count, count), 0) < iota((count, count), 1)).astype(BF16)


def split_genotypes(ref, wide):
    rows = wide.shape[0]
    wide[...] = ref[0:rows, :].astype(F32)
    return [wide[pl.ds(j, rows // 2, stride=2), :] for j in range(2)]


def select_kernel(ids, geno, sent, wide, *, shift):
    here = lax.axis_index("snp")
    blocks, pairs = ids.shape
    block = geno.shape[1]
    rows = blocks * 2 * CAP
    names = ids[...]
    local = (names & (block - 1)).astype(F32)
    hit = (lax.shift_right_logical(names, shift) == here).astype(F32)
    rank = dot(hit.astype(BF16), earlier(pairs))
    spread = (lax.shift_right_logical(iota((rows, blocks), 0), 3) == iota((rows, blocks), 1)).astype(BF16)
    hit_rows = dot(spread, hit.astype(BF16))
    rank_rows = dot(spread, rank.astype(BF16))
    local_rows = dot(spread, local.astype(BF16))
    slot = (iota((rows, pairs), 0) & (CAP - 1)).astype(F32)
    chosen = jnp.where(rank_rows == slot, hit_rows, 0.0)
    column = jnp.sum(chosen * local_rows, axis=1, keepdims=True)
    valid = jnp.sum(chosen, axis=1, keepdims=True)
    which = iota((rows, block), 1).astype(F32)
    second = (iota((rows, block), 0) & CAP) > 0
    one_hot = jnp.where((which == column) & (valid > 0.5), 1.0, 0.0)
    low = jnp.where(second, 0.0, one_hot).astype(BF16)
    high = jnp.where(second, one_hot, 0.0).astype(BF16)
    g0, g1 = split_genotypes(geno, wide)
    sent[...] = (by_t(low, g0.astype(BF16)) + by_t(high, g1.astype(BF16))).astype(BF16)


def fixed(value, samples):
    return (value * 2.0 ** (30 - (samples - 1).bit_length())).astype(jnp.int32)


def floating(value, samples):
    return value.astype(F32) * 2.0 ** ((samples - 1).bit_length() - 30)


def code_step(count):
    return jnp.maximum(count, 1.0) * (SPREAD * SPREAD / 32767.0)


def quantized(value, step):
    scaled = value * (1.0 / step)
    return jnp.clip(jnp.floor(scaled + 0.5), -32767.0, 32767.0).astype(jnp.int32)


def class_rows(label0, tail):
    case0 = label0[...].astype(F32)
    case1 = jnp.concatenate([tail[q:q + 1, :].astype(F32) for q in range(case0.shape[1] // tail.shape[1])], axis=1)
    case = jnp.concatenate([case0, case1], axis=1)
    return [case, 1.0 - case]


def coded_tiles(first_refs, second_refs, classes, left, right, wide, outs):
    k = lax.axis_index("samp")
    samples = wide.shape[0] // 2
    block = wide.shape[1]
    quarter = block // 4
    first_slab = None
    for half in range(2):
        rows = pl.ds(half * samples, samples)
        parts = split_genotypes(first_refs[half], wide)
        if half == 0:
            first_slab = [p.astype(BF16) for p in parts]
        for i in range(2):
            turned = parts[i].T
            for c in range(2):
                piece = (turned * classes[c][:, half * samples:(half + 1) * samples]).astype(BF16)
                for q in range(4):
                    d = q ^ k
                    left[d, c * 2 + i, :, rows] = piece[q * quarter:(q + 1) * quarter]
        parts = split_genotypes(second_refs[half], wide)
        for j in range(2):
            right[rows, j * block:(j + 1) * block] = parts[j].astype(BF16)
    lhs = left[...].reshape(16 * quarter, 2 * samples)
    cells = dot(lhs, right[...])
    row_sums = dot(lhs, jnp.ones((2 * samples, block), BF16))
    weights = jnp.concatenate(classes + [jnp.zeros((6, 2 * samples), F32)], axis=0).astype(BF16)
    column_sums = dot(weights, right[...])
    lanes = jnp.ones((1, 2 * block), F32)
    counts = [jnp.sum(classes[c], axis=1, keepdims=True) * lanes for c in range(2)]
    for d in range(4):
        words = None
        for c in range(2):
            rows = slice((d * 2 + c) * 2 * quarter, (d * 2 + c + 1) * 2 * quarter)
            row = row_sums[rows]
            base = jnp.concatenate([row, row], axis=1)
            centred = cells[rows] - MIDDLE * (base + column_sums[c:c + 1]) + (MIDDLE * MIDDLE) * counts[c]
            code = quantized(centred, code_step(counts[c]))
            words = lax.shift_left(code, 16) if c == 0 else words | (code & 0xFFFF)
        outs[d][0:2 * quarter, :] = words
    return first_slab, column_sums, counts


def write_tails(outs, start, samples, columns, own, counts):
    parts = [fixed(v, 2 * samples) for v in (columns[0:2], own[0:2], counts[0], counts[1])]
    tail = jnp.concatenate(parts + [jnp.zeros((2, columns.shape[1]), jnp.int32)], axis=0)
    for out in outs:
        out[start:start + 8, :] = tail


def ahead_kernel(own0, own1, other0, other1, label0, a0, a1, a2, a3, sums, wide, left, right):
    samples = wide.shape[0] // 2
    classes = class_rows(label0, own1[2 * samples:, :])
    outs = (a0, a1, a2, a3)
    _, columns, counts = coded_tiles((other0, other1), (own0, own1), classes, left, right, wide, outs)
    write_tails(outs, wide.shape[1] // 2, samples, columns, columns, counts)
    sums[...] = columns


def behind_kernel(own0, own1, other0, other1, label0, own_ids, peer_ids, got, sums,
                  b0, b1, b2, b3, wide, left, right, *, shift):
    samples = wide.shape[0] // 2
    block = wide.shape[1]
    classes = class_rows(label0, own1[2 * samples:, :])
    outs = (b0, b1, b2, b3)
    own_slab, columns, counts = coded_tiles((own0, own1), (other0, other1), classes, left, right, wide, outs)
    write_tails(outs, block // 2, samples, columns, sums[...], counts)

    pairs = peer_ids.shape[1]
    rows = got.shape[0]
    blocks = rows // (2 * CAP)
    peers = lax.shift_right_logical(peer_ids[...], shift)
    member = (iota((blocks, pairs), 0) == peers).astype(F32)
    before = dot(member.astype(BF16), earlier(pairs))
    rank = jnp.sum(member * before, axis=0, keepdims=True)
    row = iota((rows, pairs), 0)
    row_block = lax.shift_right_logical(row, 3)
    row_slot = (row & (2 * CAP - 1)).astype(F32)
    first_pick = (iota((block, pairs), 0) == own_ids[...]).astype(F32).T.astype(BF16)
    first, second = [], []
    for j in range(2):
        pick = jnp.where((row_block == peers) & (row_slot == rank + float(CAP * j)), 1.0, 0.0).T.astype(BF16)
        second.append(dot(pick, got[...]))
        first.append(by_t(first_pick, own_slab[j]))
    slab = [classes[c][:, 0:samples] for c in range(2)]
    values = []
    for c in range(2):
        for i in range(2):
            mine = first[i] * slab[c]
            for j in range(2):
                values.append(jnp.sum(mine * second[j], axis=1, keepdims=True))
    for side in (first, second):
        for c in range(2):
            for i in range(2):
                values.append(jnp.sum(side[i] * slab[c], axis=1, keepdims=True))
    lane = iota((pairs, 2 * block), 1)
    refit = jnp.zeros((pairs, 2 * block), F32)
    for v, value in enumerate(values):
        refit = jnp.where(lane == v, value, refit)
    refit = fixed(refit, 2 * samples)
    for out in outs:
        out[block // 2 + 8:, :] = refit


def complete(cells, margin_a, margin_b, totals):
    table = [[[None] * 3 for _ in range(3)] for _ in range(2)]
    for c in range(2):
        n = table[c]
        for i in range(2):
            for j in range(2):
                n[i][j] = cells[c][i][j]
            n[i][2] = margin_a[c][i] - n[i][0] - n[i][1]
        for j in range(2):
            n[2][j] = margin_b[c][j] - n[0][j] - n[1][j]
        n[2][2] = (totals[c] - margin_a[c][0] - margin_a[c][1]) - n[2][0] - n[2][1]
    return table


def kirkwood(n, margin_a, margin_b, totals):
    row_ic = [[margin_a[c][0], margin_a[c][1], totals[c] - margin_a[c][0] - margin_a[c][1]] for c in range(2)]
    col_jc = [[margin_b[c][0], margin_b[c][1], totals[c] - margin_b[c][0] - margin_b[c][1]] for c in range(2)]
    single_a = [row_ic[0][i] + row_ic[1][i] for i in range(3)]
    single_b = [col_jc[0][j] + col_jc[1][j] for j in range(3)]
    grand = totals[0] + totals[1]
    inv_a = [1.0 / s for s in single_a]
    row_x = [[row_ic[c][i] * inv_a[i] / totals[c] for i in range(3)] for c in range(2)]
    col_y = [[col_jc[c][j] / single_b[j] for j in range(3)] for c in range(2)]
    scale = None
    approx = {}
    for i in range(3):
        for j in range(3):
            pair = n[0][i][j] + n[1][i][j]
            for c in range(2):
                value = pair * row_x[c][i] * col_y[c][j]
                approx[c, i, j] = value
                scale = value if scale is None else scale + value
    factor = scale / grand
    total = None
    for (c, i, j), value in approx.items():
        term = n[c][i][j] * jnp.log(n[c][i][j] * factor / value)
        total = term if total is None else total + term
    return 2.0 * total


def finish_kernel(b0, b1, b2, b3, a0, a1, a2, a3, screen, stat, columns, *, samples):
    k = lax.axis_index("samp")
    bs, as_ = (b0, b1, b2, b3), (a0, a1, a2, a3)
    block = b0.shape[1] // 2
    quarter = block // 4
    height = 2 * quarter
    pairs = stat.shape[1]

    def both(x, y, row, lanes=slice(0, block)):
        return floating(x[row:row + 1, lanes], 2 * samples) + floating(y[row:row + 1, lanes], 2 * samples)

    lanes_of = [slice(j * block, (j + 1) * block) for j in range(2)]
    totals_row = [both(b0, b2, height + 4 + c) for c in range(2)]
    own = [both(b0, b2, height + 2 + c, lanes_of[i]) for c in range(2) for i in range(2)]
    columns[...] = jnp.concatenate(own + [jnp.zeros((block - 4, block), F32)], axis=0).T
    mine = columns[pl.ds(pl.multiple_of(k * quarter, quarter), quarter), :]
    margin_a = [[jnp.broadcast_to(mine[:, c * 2 + i:c * 2 + i + 1], (quarter, block)) for i in range(2)] for c in range(2)]

    stats = []
    for msgs in (bs, as_):
        for parity in range(2):
            x, y = msgs[parity], msgs[parity + 2]
            steps = [[code_step(floating(m[height + 4 + c:height + 5 + c, 0:block], 2 * samples)) for m in (x, y)]
                     for c in range(2)]
            margin_b = [[both(x, y, height + c, lanes_of[j]) for j in range(2)] for c in range(2)]
            cells = [[[None, None], [None, None]] for _ in range(2)]
            for i in range(2):
                for j in range(2):
                    words = [m[i * quarter:(i + 1) * quarter, lanes_of[j]] for m in (x, y)]
                    for c in range(2):
                        codes = [lax.shift_right_arithmetic(w if c == 0 else lax.shift_left(w, 16), 16) for w in words]
                        base = MIDDLE * (margin_a[c][i] + margin_b[c][j]) - (MIDDLE * MIDDLE) * totals_row[c]
                        cells[c][i][j] = (codes[0].astype(F32) * steps[c][0] + codes[1].astype(F32) * steps[c][1]) + base
            table = complete(cells, margin_a, margin_b, totals_row)
            stats.append(kirkwood(table, margin_a, margin_b, totals_row))
    even = (k & 1) == 0
    for side in range(2):
        e, o = stats[2 * side], stats[2 * side + 1]
        screen[:, 2 * side, :] = jnp.where(even, e, o)
        screen[:, 2 * side + 1, :] = jnp.where(even, o, e)

    for start in range(0, pairs, block):
        count = min(block, pairs - start)
        rows = slice(height + 8 + start, height + 8 + start + count)
        sums = floating(b0[rows, 0:block] + b1[rows, 0:block] + b2[rows, 0:block] + b3[rows, 0:block], 2 * samples)
        if count < block:
            sums = jnp.concatenate([sums, jnp.ones((block - count, block), F32)], axis=0)
        turned = sums.T
        row = [turned[v:v + 1, :] for v in range(16)]
        cells = [[[row[c * 4 + i * 2 + j] for j in range(2)] for i in range(2)] for c in range(2)]
        ma = [[row[8 + c * 2 + i] for i in range(2)] for c in range(2)]
        mb = [[row[12 + c * 2 + j] for j in range(2)] for c in range(2)]
        n = complete(cells, ma, mb, totals_row)
        n_ij = [[n[0][i][j] + n[1][i][j] for j in range(3)] for i in range(3)]
        n_ic = [[n[c][i][0] + n[c][i][1] + n[c][i][2] for i in range(3)] for c in range(2)]
        n_jc = [[n[c][0][j] + n[c][1][j] + n[c][2][j] for j in range(3)] for c in range(2)]

        def sweep(_, flat):
            f = [[[flat[c * 9 + i * 3 + j] for j in range(3)] for i in range(3)] for c in range(2)]
            for i in range(3):
                for j in range(3):
                    ratio = n_ij[i][j] / (f[0][i][j] + f[1][i][j])
                    for c in range(2):
                        f[c][i][j] = f[c][i][j] * ratio
            for c in range(2):
                for i in range(3):
                    ratio = n_ic[c][i] / (f[c][i][0] + f[c][i][1] + f[c][i][2])
                    for j in range(3):
                        f[c][i][j] = f[c][i][j] * ratio
                for j in range(3):
                    ratio = n_jc[c][j] / (f[c][0][j] + f[c][1][j] + f[c][2][j])
                    for i in range(3):
                        f[c][i][j] = f[c][i][j] * ratio
            return tuple(f[c][i][j] for c in range(2) for i in range(3) for j in range(3))

        fitted = lax.fori_loop(0, ITERS, sweep, tuple(jnp.ones((1, block), F32) for _ in range(18)))
        total = None
        for c in range(2):
            for i in range(3):
                for j in range(3):
                    term = n[c][i][j] * jnp.log(n[c][i][j] / fitted[c * 9 + i * 3 + j])
                    total = term if total is None else total + term
        stat[:, start:start + count] = (2.0 * total)[:, 0:count]


def vmem(count):
    return [pl.BlockSpec(memory_space=pltpu.VMEM)] * count


def run(body, args, outs, scratch, near=True):
    return pl.pallas_call(
        body,
        out_shape=[pltpu.VMEM(o.shape, o.dtype) if near else o for o in outs],
        in_specs=vmem(len(args)),
        out_specs=vmem(len(outs)),
        scratch_shapes=scratch,
    )(*(pltpu.with_memory_space_constraint(a, pltpu.VMEM) for a in args))


def mark_kernel(geno, label0, out):
    rows, block = geno.shape
    out[0:rows, :] = geno[...]
    case = label0[...].astype(F32)
    parts = [case[:, q * block:(q + 1) * block] for q in range(case.shape[1] // block)]
    parts.append(jnp.zeros((out.shape[0] - rows - len(parts), block), F32))
    out[rows:, :] = jnp.concatenate(parts, axis=0).astype(BF16)


def on_device(genotypes, case_labels, refit_own, refit_peer):
    samples, _, block = genotypes.shape
    pairs = refit_peer.shape[0]
    snp_count = lax.axis_size("snp")
    samp_count = lax.axis_size("samp")
    assert samp_count == 2 * HALF and block & (block - 1) == 0
    shift = block.bit_length() - 1
    here = lax.axis_index("snp")

    def moved(value, where):
        links = []
        for b in range(snp_count):
            for k in range(samp_count):
                to_b, to_k = where(b, k)
                links.append((b * samp_count + k, (to_b % snp_count) * samp_count + to_k % samp_count))
        return lax.ppermute(value, ("snp", "samp"), links)

    geno = genotypes.reshape(2 * samples, block)
    labels = case_labels.reshape(1, samples)
    (marked,) = run(
        mark_kernel, (geno, labels),
        [jax.ShapeDtypeStruct((2 * samples + samples // block + -(samples // block) % 8, block), BF16)], [],
    )
    other0 = moved(geno, lambda b, k: (b + 1 + (k & 1), k))
    other1 = moved(geno, lambda b, k: (b + 2 - (k & 1), k ^ 1))
    own1 = moved(marked, lambda b, k: (b, k ^ 1))
    ids = lax.psum(jnp.where(iota((snp_count, pairs), 0) == here, refit_peer[None, :], 0), "snp")
    wide = pltpu.VMEM((2 * samples, block), F32)
    (sent,) = run(
        functools.partial(select_kernel, shift=shift), (ids, geno),
        [jax.ShapeDtypeStruct((snp_count * 2 * CAP, samples), BF16)], [wide],
    )
    got = lax.all_to_all(sent, "snp", split_axis=0, concat_axis=0, tiled=True)
    scratch = [wide, pltpu.VMEM((4, 4, block // 4, 2 * samples), BF16), pltpu.VMEM((2 * samples, 2 * block), BF16)]
    short = jax.ShapeDtypeStruct((block // 2 + 8, 2 * block), jnp.int32)
    tall = jax.ShapeDtypeStruct((block // 2 + 8 + pairs, 2 * block), jnp.int32)
    *ahead, sums = run(
        ahead_kernel, (geno, own1, other0, other1, labels),
        [short] * 4 + [jax.ShapeDtypeStruct((8, 2 * block), F32)], scratch,
    )
    for d in range(4):
        ahead[d] = moved(ahead[d], lambda b, k: (b - 1 - (k & 1), k ^ d))
    behind = run(
        functools.partial(behind_kernel, shift=shift),
        (geno, own1, other0, other1, labels, refit_own[None, :], refit_peer[None, :], got, sums),
        [tall] * 4, scratch,
    )
    behind = list(behind)
    for d in range(1, 4):
        behind[d] = moved(behind[d], lambda b, k: (b, k ^ d))
    screen, stat = run(
        functools.partial(finish_kernel, samples=samples), (*behind, *ahead),
        [jax.ShapeDtypeStruct((block // samp_count, 2 * HALF, block), F32), jax.ShapeDtypeStruct((1, pairs), F32)],
        [pltpu.VMEM((block, block), F32)], near=False,
    )
    return screen, stat.reshape(pairs)


def solution(mesh):
    in_specs = (P("samp", None, "snp"), P("samp"), P("snp"), P("snp"))
    out_specs = (P(("snp", "samp"), None, None), P("snp"))

    return jax.shard_map(on_device, mesh=mesh, in_specs=in_specs, out_specs=out_specs, check_vma=False)
```

```python
import functools

import jax
import jax.numpy as jnp
from jax import lax
from jax.experimental import pallas as pl
from jax.experimental.pallas import tpu as pltpu
from jax.sharding import PartitionSpec as P

HALF = 2
CAP = 4
ITERS = 10
MIDDLE = 0.47
SPREAD = 0.411
F32 = jnp.float32
BF16 = jnp.bfloat16


def iota(shape, axis):
    return lax.broadcasted_iota(jnp.int32, shape, axis)


def by_t(a, b):
    return lax.dot_general(a, b, (((1,), (1,)), ((), ())), preferred_element_type=F32)


def dot(a, b):
    return lax.dot_general(a, b, (((1,), (0,)), ((), ())), preferred_element_type=F32)


def earlier(count):
    return (iota((count, count), 0) < iota((count, count), 1)).astype(BF16)


def split_genotypes(ref, wide):
    rows = wide.shape[0]
    wide[...] = ref[0:rows, :].astype(F32)
    return [wide[pl.ds(j, rows // 2, stride=2), :] for j in range(2)]


def select_kernel(ids, geno, sent, wide, *, shift):
    here = lax.axis_index("snp")
    blocks, pairs = ids.shape
    block = geno.shape[1]
    rows = blocks * 2 * CAP
    names = ids[...]
    local = (names & (block - 1)).astype(F32)
    hit = (lax.shift_right_logical(names, shift) == here).astype(F32)
    rank = dot(hit.astype(BF16), earlier(pairs))
    spread = (lax.shift_right_logical(iota((rows, blocks), 0), 3) == iota((rows, blocks), 1)).astype(BF16)
    hit_rows = dot(spread, hit.astype(BF16))
    rank_rows = dot(spread, rank.astype(BF16))
    local_rows = dot(spread, local.astype(BF16))
    slot = (iota((rows, pairs), 0) & (CAP - 1)).astype(F32)
    chosen = jnp.where(rank_rows == slot, hit_rows, 0.0)
    column = jnp.sum(chosen * local_rows, axis=1, keepdims=True)
    valid = jnp.sum(chosen, axis=1, keepdims=True)
    which = iota((rows, block), 1).astype(F32)
    second = (iota((rows, block), 0) & CAP) > 0
    one_hot = jnp.where((which == column) & (valid > 0.5), 1.0, 0.0)
    low = jnp.where(second, 0.0, one_hot).astype(BF16)
    high = jnp.where(second, one_hot, 0.0).astype(BF16)
    g0, g1 = split_genotypes(geno, wide)
    sent[...] = (by_t(low, g0.astype(BF16)) + by_t(high, g1.astype(BF16))).astype(BF16)


def fixed(value, samples):
    return (value * 2.0 ** (30 - (samples - 1).bit_length())).astype(jnp.int32)


def floating(value, samples):
    return value.astype(F32) * 2.0 ** ((samples - 1).bit_length() - 30)


def code_step(count):
    return jnp.maximum(count, 1.0) * (SPREAD * SPREAD / 32767.0)


def quantized(value, step):
    scaled = value * (1.0 / step)
    return jnp.clip(jnp.floor(scaled + 0.5), -32767.0, 32767.0).astype(jnp.int32)


def class_rows(label0, tail):
    case0 = label0[...].astype(F32)
    case1 = jnp.concatenate([tail[q:q + 1, :].astype(F32) for q in range(case0.shape[1] // tail.shape[1])], axis=1)
    case = jnp.concatenate([case0, case1], axis=1)
    return [case, 1.0 - case]


def coded_tiles(first_refs, second_refs, classes, left, right, wide, outs):
    k = lax.axis_index("samp")
    samples = wide.shape[0] // 2
    block = wide.shape[1]
    quarter = block // 4
    first_slab = None
    for half in range(2):
        rows = pl.ds(half * samples, samples)
        parts = split_genotypes(first_refs[half], wide)
        if half == 0:
            first_slab = [p.astype(BF16) for p in parts]
        for i in range(2):
            turned = parts[i].T
            for c in range(2):
                piece = (turned * classes[c][:, half * samples:(half + 1) * samples]).astype(BF16)
                for q in range(4):
                    d = q ^ k
                    left[d, c * 2 + i, :, rows] = piece[q * quarter:(q + 1) * quarter]
        parts = split_genotypes(second_refs[half], wide)
        for j in range(2):
            right[rows, j * block:(j + 1) * block] = parts[j].astype(BF16)
    lhs = left[...].reshape(16 * quarter, 2 * samples)
    cells = dot(lhs, right[...])
    row_sums = dot(lhs, jnp.ones((2 * samples, block), BF16))
    weights = jnp.concatenate(classes + [jnp.zeros((6, 2 * samples), F32)], axis=0).astype(BF16)
    column_sums = dot(weights, right[...])
    lanes = jnp.ones((1, 2 * block), F32)
    counts = [jnp.sum(classes[c], axis=1, keepdims=True) * lanes for c in range(2)]
    for d in range(4):
        words = None
        for c in range(2):
            rows = slice((d * 2 + c) * 2 * quarter, (d * 2 + c + 1) * 2 * quarter)
            row = row_sums[rows]
            base = jnp.concatenate([row, row], axis=1)
            centred = cells[rows] - MIDDLE * (base + column_sums[c:c + 1]) + (MIDDLE * MIDDLE) * counts[c]
            code = quantized(centred, code_step(counts[c]))
            words = lax.shift_left(code, 16) if c == 0 else words | (code & 0xFFFF)
        outs[d][0:2 * quarter, :] = words
    return first_slab, column_sums, counts


def write_tails(outs, start, samples, columns, own, counts):
    parts = [fixed(v, 2 * samples) for v in (columns[0:2], own[0:2], counts[0], counts[1])]
    tail = jnp.concatenate(parts + [jnp.zeros((2, columns.shape[1]), jnp.int32)], axis=0)
    for out in outs:
        out[start:start + 8, :] = tail


def ahead_kernel(own0, own1, other0, other1, label0, a0, a1, a2, a3, sums, wide, left, right):
    samples = wide.shape[0] // 2
    classes = class_rows(label0, own1[2 * samples:, :])
    outs = (a0, a1, a2, a3)
    _, columns, counts = coded_tiles((other0, other1), (own0, own1), classes, left, right, wide, outs)
    write_tails(outs, wide.shape[1] // 2, samples, columns, columns, counts)
    sums[...] = columns


def behind_kernel(own0, own1, other0, other1, label0, own_ids, peer_ids, got, sums,
                  b0, b1, b2, b3, wide, left, right, *, shift):
    samples = wide.shape[0] // 2
    block = wide.shape[1]
    classes = class_rows(label0, own1[2 * samples:, :])
    outs = (b0, b1, b2, b3)
    own_slab, columns, counts = coded_tiles((own0, own1), (other0, other1), classes, left, right, wide, outs)
    write_tails(outs, block // 2, samples, columns, sums[...], counts)

    pairs = peer_ids.shape[1]
    rows = got.shape[0]
    blocks = rows // (2 * CAP)
    peers = lax.shift_right_logical(peer_ids[...], shift)
    member = (iota((blocks, pairs), 0) == peers).astype(F32)
    before = dot(member.astype(BF16), earlier(pairs))
    rank = jnp.sum(member * before, axis=0, keepdims=True)
    row = iota((rows, pairs), 0)
    row_block = lax.shift_right_logical(row, 3)
    row_slot = (row & (2 * CAP - 1)).astype(F32)
    first_pick = (iota((block, pairs), 0) == own_ids[...]).astype(F32).T.astype(BF16)
    first, second = [], []
    for j in range(2):
        pick = jnp.where((row_block == peers) & (row_slot == rank + float(CAP * j)), 1.0, 0.0).T.astype(BF16)
        second.append(dot(pick, got[...]))
        first.append(by_t(first_pick, own_slab[j]))
    slab = [classes[c][:, 0:samples] for c in range(2)]
    values = []
    for c in range(2):
        for i in range(2):
            mine = first[i] * slab[c]
            for j in range(2):
                values.append(jnp.sum(mine * second[j], axis=1, keepdims=True))
    for side in (first, second):
        for c in range(2):
            for i in range(2):
                values.append(jnp.sum(side[i] * slab[c], axis=1, keepdims=True))
    lane = iota((pairs, 2 * block), 1)
    refit = jnp.zeros((pairs, 2 * block), F32)
    for v, value in enumerate(values):
        refit = jnp.where(lane == v, value, refit)
    refit = fixed(refit, 2 * samples)
    for out in outs:
        out[block // 2 + 8:, :] = refit


def complete(cells, margin_a, margin_b, totals):
    table = [[[None] * 3 for _ in range(3)] for _ in range(2)]
    for c in range(2):
        n = table[c]
        for i in range(2):
            for j in range(2):
                n[i][j] = cells[c][i][j]
            n[i][2] = margin_a[c][i] - n[i][0] - n[i][1]
        for j in range(2):
            n[2][j] = margin_b[c][j] - n[0][j] - n[1][j]
        n[2][2] = (totals[c] - margin_a[c][0] - margin_a[c][1]) - n[2][0] - n[2][1]
    return table


def kirkwood(n, margin_a, margin_b, totals):
    row_ic = [[margin_a[c][0], margin_a[c][1], totals[c] - margin_a[c][0] - margin_a[c][1]] for c in range(2)]
    col_jc = [[margin_b[c][0], margin_b[c][1], totals[c] - margin_b[c][0] - margin_b[c][1]] for c in range(2)]
    single_a = [row_ic[0][i] + row_ic[1][i] for i in range(3)]
    single_b = [col_jc[0][j] + col_jc[1][j] for j in range(3)]
    grand = totals[0] + totals[1]
    inv_a = [1.0 / s for s in single_a]
    row_x = [[row_ic[c][i] * inv_a[i] / totals[c] for i in range(3)] for c in range(2)]
    col_y = [[col_jc[c][j] / single_b[j] for j in range(3)] for c in range(2)]
    scale = None
    approx = {}
    for i in range(3):
        for j in range(3):
            pair = n[0][i][j] + n[1][i][j]
            for c in range(2):
                value = pair * row_x[c][i] * col_y[c][j]
                approx[c, i, j] = value
                scale = value if scale is None else scale + value
    factor = scale / grand
    total = None
    for (c, i, j), value in approx.items():
        term = n[c][i][j] * jnp.log(n[c][i][j] * factor / value)
        total = term if total is None else total + term
    return 2.0 * total


def finish_kernel(b0, b1, b2, b3, a0, a1, a2, a3, screen, stat, columns, *, samples):
    k = lax.axis_index("samp")
    bs, as_ = (b0, b1, b2, b3), (a0, a1, a2, a3)
    block = b0.shape[1] // 2
    quarter = block // 4
    height = 2 * quarter
    pairs = stat.shape[1]

    def both(x, y, row, lanes=slice(0, block)):
        return floating(x[row:row + 1, lanes], 2 * samples) + floating(y[row:row + 1, lanes], 2 * samples)

    lanes_of = [slice(j * block, (j + 1) * block) for j in range(2)]
    totals_row = [both(b0, b2, height + 4 + c) for c in range(2)]
    own = [both(b0, b2, height + 2 + c, lanes_of[i]) for c in range(2) for i in range(2)]
    columns[...] = jnp.concatenate(own + [jnp.zeros((block - 4, block), F32)], axis=0).T
    mine = columns[pl.ds(pl.multiple_of(k * quarter, quarter), quarter), :]
    margin_a = [[jnp.broadcast_to(mine[:, c * 2 + i:c * 2 + i + 1], (quarter, block)) for i in range(2)] for c in range(2)]

    stats = []
    for msgs in (bs, as_):
        for parity in range(2):
            x, y = msgs[parity], msgs[parity + 2]
            steps = [[code_step(floating(m[height + 4 + c:height + 5 + c, 0:block], 2 * samples)) for m in (x, y)]
                     for c in range(2)]
            margin_b = [[both(x, y, height + c, lanes_of[j]) for j in range(2)] for c in range(2)]
            cells = [[[None, None], [None, None]] for _ in range(2)]
            for i in range(2):
                for j in range(2):
                    words = [m[i * quarter:(i + 1) * quarter, lanes_of[j]] for m in (x, y)]
                    for c in range(2):
                        codes = [lax.shift_right_arithmetic(w if c == 0 else lax.shift_left(w, 16), 16) for w in words]
                        base = MIDDLE * (margin_a[c][i] + margin_b[c][j]) - (MIDDLE * MIDDLE) * totals_row[c]
                        cells[c][i][j] = (codes[0].astype(F32) * steps[c][0] + codes[1].astype(F32) * steps[c][1]) + base
            table = complete(cells, margin_a, margin_b, totals_row)
            stats.append(kirkwood(table, margin_a, margin_b, totals_row))
    even = (k & 1) == 0
    for side in range(2):
        e, o = stats[2 * side], stats[2 * side + 1]
        screen[:, 2 * side, :] = jnp.where(even, e, o)
        screen[:, 2 * side + 1, :] = jnp.where(even, o, e)

    for start in range(0, pairs, block):
        count = min(block, pairs - start)
        rows = slice(height + 8 + start, height + 8 + start + count)
        sums = floating(b0[rows, 0:block] + b1[rows, 0:block] + b2[rows, 0:block] + b3[rows, 0:block], 2 * samples)
        if count < block:
            sums = jnp.concatenate([sums, jnp.ones((block - count, block), F32)], axis=0)
        turned = sums.T
        row = [turned[v:v + 1, :] for v in range(16)]
        cells = [[[row[c * 4 + i * 2 + j] for j in range(2)] for i in range(2)] for c in range(2)]
        ma = [[row[8 + c * 2 + i] for i in range(2)] for c in range(2)]
        mb = [[row[12 + c * 2 + j] for j in range(2)] for c in range(2)]
        n = complete(cells, ma, mb, totals_row)
        n_ij = [[n[0][i][j] + n[1][i][j] for j in range(3)] for i in range(3)]
        n_ic = [[n[c][i][0] + n[c][i][1] + n[c][i][2] for i in range(3)] for c in range(2)]
        n_jc = [[n[c][0][j] + n[c][1][j] + n[c][2][j] for j in range(3)] for c in range(2)]

        def sweep(_, flat):
            f = [[[flat[c * 9 + i * 3 + j] for j in range(3)] for i in range(3)] for c in range(2)]
            for i in range(3):
                for j in range(3):
                    ratio = n_ij[i][j] / (f[0][i][j] + f[1][i][j])
                    for c in range(2):
                        f[c][i][j] = f[c][i][j] * ratio
            for c in range(2):
                for i in range(3):
                    ratio = n_ic[c][i] / (f[c][i][0] + f[c][i][1] + f[c][i][2])
                    for j in range(3):
                        f[c][i][j] = f[c][i][j] * ratio
                for j in range(3):
                    ratio = n_jc[c][j] / (f[c][0][j] + f[c][1][j] + f[c][2][j])
                    for i in range(3):
                        f[c][i][j] = f[c][i][j] * ratio
            return tuple(f[c][i][j] for c in range(2) for i in range(3) for j in range(3))

        fitted = lax.fori_loop(0, ITERS, sweep, tuple(jnp.ones((1, block), F32) for _ in range(18)))
        total = None
        for c in range(2):
            for i in range(3):
                for j in range(3):
                    term = n[c][i][j] * jnp.log(n[c][i][j] / fitted[c * 9 + i * 3 + j])
                    total = term if total is None else total + term
        stat[:, start:start + count] = (2.0 * total)[:, 0:count]


def vmem(count):
    return [pl.BlockSpec(memory_space=pltpu.VMEM)] * count


def run(body, args, outs, scratch, near=True):
    return pl.pallas_call(
        body,
        out_shape=[pltpu.VMEM(o.shape, o.dtype) if near else o for o in outs],
        in_specs=vmem(len(args)),
        out_specs=vmem(len(outs)),
        scratch_shapes=scratch,
    )(*(pltpu.with_memory_space_constraint(a, pltpu.VMEM) for a in args))


def stage_kernel(geno, label0, own_ids, peer_ids, out, label_copy, own_copy, peer_copy, placed, sems):
    rows, block = geno.shape
    copies = [
        pltpu.make_async_copy(src, dst, sems.at[n])
        for n, (src, dst) in enumerate(((geno, out.at[0:rows]), (label0, label_copy), (own_ids, own_copy), (peer_ids, peer_copy)))
    ]
    for copy in copies:
        copy.start()
    for copy in copies[1:]:
        copy.wait()
    placed[...] = jnp.where(iota(placed.shape, 0) == lax.axis_index("snp"), peer_copy[...], 0)
    case = label_copy[...].astype(F32)
    parts = [case[:, q * block:(q + 1) * block] for q in range(case.shape[1] // block)]
    parts.append(jnp.zeros((out.shape[0] - rows - len(parts), block), F32))
    out[rows:, :] = jnp.concatenate(parts, axis=0).astype(BF16)
    copies[0].wait()


def on_device(genotypes, case_labels, refit_own, refit_peer):
    samples, _, block = genotypes.shape
    pairs = refit_peer.shape[0]
    snp_count = lax.axis_size("snp")
    samp_count = lax.axis_size("samp")
    assert samp_count == 2 * HALF and block & (block - 1) == 0
    shift = block.bit_length() - 1

    def moved(value, where):
        links = []
        for b in range(snp_count):
            for k in range(samp_count):
                to_b, to_k = where(b, k)
                links.append((b * samp_count + k, (to_b % snp_count) * samp_count + to_k % samp_count))
        return lax.ppermute(value, ("snp", "samp"), links)

    geno = genotypes.reshape(2 * samples, block)
    labels = case_labels.reshape(1, samples)
    row_of = lambda count: pltpu.VMEM((1, count), jnp.int32)
    height = 2 * samples + samples // block + -(samples // block) % 8
    marked, labels, own_ids, peer_ids, placed = pl.pallas_call(
        stage_kernel,
        out_shape=[pltpu.VMEM((height, block), BF16), row_of(samples), row_of(pairs), row_of(pairs),
                   pltpu.VMEM((snp_count, pairs), jnp.int32)],
        in_specs=[pl.BlockSpec(memory_space=pl.ANY)] * 4,
        out_specs=vmem(5),
        scratch_shapes=[pltpu.SemaphoreType.DMA((4,))],
    )(geno, labels, refit_own[None, :], refit_peer[None, :])
    other0 = moved(geno, lambda b, k: (b + 1 + (k & 1), k))
    other1 = moved(geno, lambda b, k: (b + 2 - (k & 1), k ^ 1))
    own1 = moved(marked, lambda b, k: (b, k ^ 1))
    ids = lax.psum(placed, "snp")
    wide = pltpu.VMEM((2 * samples, block), F32)
    (sent,) = run(
        functools.partial(select_kernel, shift=shift), (ids, marked),
        [jax.ShapeDtypeStruct((snp_count * 2 * CAP, samples), BF16)], [wide],
    )
    got = lax.all_to_all(sent, "snp", split_axis=0, concat_axis=0, tiled=True)
    scratch = [wide, pltpu.VMEM((4, 4, block // 4, 2 * samples), BF16), pltpu.VMEM((2 * samples, 2 * block), BF16)]
    short = jax.ShapeDtypeStruct((block // 2 + 8, 2 * block), jnp.int32)
    tall = jax.ShapeDtypeStruct((block // 2 + 8 + pairs, 2 * block), jnp.int32)
    *ahead, sums = run(
        ahead_kernel, (marked, own1, other0, other1, labels),
        [short] * 4 + [jax.ShapeDtypeStruct((8, 2 * block), F32)], scratch,
    )
    for d in range(4):
        ahead[d] = moved(ahead[d], lambda b, k: (b - 1 - (k & 1), k ^ d))
    behind = run(
        functools.partial(behind_kernel, shift=shift),
        (marked, own1, other0, other1, labels, own_ids, peer_ids, got, sums),
        [tall] * 4, scratch,
    )
    behind = list(behind)
    for d in range(1, 4):
        behind[d] = moved(behind[d], lambda b, k: (b, k ^ d))
    screen, stat = run(
        functools.partial(finish_kernel, samples=samples), (*behind, *ahead),
        [jax.ShapeDtypeStruct((block // samp_count, 2 * HALF, block), F32), jax.ShapeDtypeStruct((1, pairs), F32)],
        [pltpu.VMEM((block, block), F32)], near=False,
    )
    return screen, stat.reshape(pairs)


def solution(mesh):
    in_specs = (P("samp", None, "snp"), P("samp"), P("snp"), P("snp"))
    out_specs = (P(("snp", "samp"), None, None), P("snp"))

    return jax.shard_map(on_device, mesh=mesh, in_specs=in_specs, out_specs=out_specs, check_vma=False)
```

```python
import functools

import jax
import jax.numpy as jnp
from jax import lax
from jax.experimental import pallas as pl
from jax.experimental.pallas import tpu as pltpu
from jax.sharding import PartitionSpec as P

HALF = 2
CAP = 4
ITERS = 10
MIDDLE = 0.47
SPREAD = 0.411
F32 = jnp.float32
BF16 = jnp.bfloat16


def iota(shape, axis):
    return lax.broadcasted_iota(jnp.int32, shape, axis)


def by_t(a, b):
    return lax.dot_general(a, b, (((1,), (1,)), ((), ())), preferred_element_type=F32)


def dot(a, b):
    return lax.dot_general(a, b, (((1,), (0,)), ((), ())), preferred_element_type=F32)


def earlier(count):
    return (iota((count, count), 0) < iota((count, count), 1)).astype(BF16)


def split_genotypes(ref, wide):
    rows = wide.shape[0]
    wide[...] = ref[0:rows, :].astype(F32)
    return [wide[pl.ds(j, rows // 2, stride=2), :] for j in range(2)]


def select_kernel(ids, geno, sent, wide, *, shift):
    here = lax.axis_index("snp")
    blocks, pairs = ids.shape
    block = geno.shape[1]
    rows = blocks * 2 * CAP
    names = ids[...]
    local = (names & (block - 1)).astype(F32)
    hit = (lax.shift_right_logical(names, shift) == here).astype(F32)
    rank = dot(hit.astype(BF16), earlier(pairs))
    spread = (lax.shift_right_logical(iota((rows, blocks), 0), 3) == iota((rows, blocks), 1)).astype(BF16)
    hit_rows = dot(spread, hit.astype(BF16))
    rank_rows = dot(spread, rank.astype(BF16))
    local_rows = dot(spread, local.astype(BF16))
    slot = (iota((rows, pairs), 0) & (CAP - 1)).astype(F32)
    chosen = jnp.where(rank_rows == slot, hit_rows, 0.0)
    column = jnp.sum(chosen * local_rows, axis=1, keepdims=True)
    valid = jnp.sum(chosen, axis=1, keepdims=True)
    which = iota((rows, block), 1).astype(F32)
    second = (iota((rows, block), 0) & CAP) > 0
    one_hot = jnp.where((which == column) & (valid > 0.5), 1.0, 0.0)
    low = jnp.where(second, 0.0, one_hot).astype(BF16)
    high = jnp.where(second, one_hot, 0.0).astype(BF16)
    g0, g1 = split_genotypes(geno, wide)
    sent[...] = (by_t(low, g0.astype(BF16)) + by_t(high, g1.astype(BF16))).astype(BF16)


def fixed(value, samples):
    return (value * 2.0 ** (30 - (samples - 1).bit_length())).astype(jnp.int32)


def floating(value, samples):
    return value.astype(F32) * 2.0 ** ((samples - 1).bit_length() - 30)


def code_step(count):
    return jnp.maximum(count, 1.0) * (SPREAD * SPREAD / 32767.0)


def quantized(value, step):
    scaled = value * (1.0 / step)
    return jnp.clip(jnp.floor(scaled + 0.5), -32767.0, 32767.0).astype(jnp.int32)


def class_rows(label0, tail):
    case0 = label0[...].astype(F32)
    case1 = jnp.concatenate([tail[q:q + 1, :].astype(F32) for q in range(case0.shape[1] // tail.shape[1])], axis=1)
    case = jnp.concatenate([case0, case1], axis=1)
    return [case, 1.0 - case]


def coded_tiles(first_refs, second_refs, classes, left, right, wide, outs):
    k = lax.axis_index("samp")
    samples = wide.shape[0] // 2
    block = wide.shape[1]
    quarter = block // 4
    first_slab = None
    for half in range(2):
        rows = pl.ds(half * samples, samples)
        parts = split_genotypes(first_refs[half], wide)
        if half == 0:
            first_slab = [p.astype(BF16) for p in parts]
        for i in range(2):
            turned = parts[i].T
            for c in range(2):
                piece = (turned * classes[c][:, half * samples:(half + 1) * samples]).astype(BF16)
                for q in range(4):
                    d = q ^ k
                    left[d, c * 2 + i, :, rows] = piece[q * quarter:(q + 1) * quarter]
        parts = split_genotypes(second_refs[half], wide)
        for j in range(2):
            right[rows, j * block:(j + 1) * block] = parts[j].astype(BF16)
    lhs = left[...].reshape(16 * quarter, 2 * samples)
    cells = dot(lhs, right[...])
    row_sums = dot(lhs, jnp.ones((2 * samples, block), BF16))
    weights = jnp.concatenate(classes + [jnp.zeros((6, 2 * samples), F32)], axis=0).astype(BF16)
    column_sums = dot(weights, right[...])
    lanes = jnp.ones((1, 2 * block), F32)
    counts = [jnp.sum(classes[c], axis=1, keepdims=True) * lanes for c in range(2)]
    for d in range(4):
        words = None
        for c in range(2):
            rows = slice((d * 2 + c) * 2 * quarter, (d * 2 + c + 1) * 2 * quarter)
            row = row_sums[rows]
            base = jnp.concatenate([row, row], axis=1)
            centred = cells[rows] - MIDDLE * (base + column_sums[c:c + 1]) + (MIDDLE * MIDDLE) * counts[c]
            code = quantized(centred, code_step(counts[c]))
            words = lax.shift_left(code, 16) if c == 0 else words | (code & 0xFFFF)
        for j in range(2):
            outs[d][j * 2 * quarter:(j + 1) * 2 * quarter, :] = words[:, j * block:(j + 1) * block]
    return first_slab, column_sums, counts


def write_tails(outs, samples, block, groups):
    rows = []
    for group in groups:
        for row in group:
            rows += [row[:, j:j + block] for j in range(0, row.shape[1], block)]
    rows.append(jnp.zeros((8 - len(rows), block), F32))
    tail = fixed(jnp.concatenate(rows[:-1] if len(rows) == 9 else rows, axis=0), 2 * samples)
    for out in outs:
        out[block:block + 8, :] = tail


def ahead_kernel(own0, own1, other0, other1, label0, a0, a1, a2, a3, sums, wide, left, right):
    samples = wide.shape[0] // 2
    classes = class_rows(label0, own1[2 * samples:, :])
    outs = (a0, a1, a2, a3)
    _, columns, counts = coded_tiles((other0, other1), (own0, own1), classes, left, right, wide, outs)
    block = wide.shape[1]
    write_tails(outs, samples, block, ((columns[0:1], columns[1:2]), (counts[0][:, 0:block], counts[1][:, 0:block])))
    sums[...] = columns


def behind_kernel(own0, own1, other0, other1, label0, own_ids, peer_ids, got, sums,
                  b0, b1, b2, b3, wide, left, right, *, shift):
    samples = wide.shape[0] // 2
    block = wide.shape[1]
    classes = class_rows(label0, own1[2 * samples:, :])
    outs = (b0, b1, b2, b3)
    own_slab, columns, counts = coded_tiles((own0, own1), (other0, other1), classes, left, right, wide, outs)
    write_tails(outs, samples, block, ((columns[0:1], columns[1:2]), (sums[0:1, :], sums[1:2, :])))

    pairs = peer_ids.shape[1]
    rows = got.shape[0]
    blocks = rows // (2 * CAP)
    peers = lax.shift_right_logical(peer_ids[...], shift)
    member = (iota((blocks, pairs), 0) == peers).astype(F32)
    before = dot(member.astype(BF16), earlier(pairs))
    rank = jnp.sum(member * before, axis=0, keepdims=True)
    row = iota((rows, pairs), 0)
    row_block = lax.shift_right_logical(row, 3)
    row_slot = (row & (2 * CAP - 1)).astype(F32)
    first_pick = (iota((block, pairs), 0) == own_ids[...]).astype(F32).T.astype(BF16)
    first, second = [], []
    for j in range(2):
        pick = jnp.where((row_block == peers) & (row_slot == rank + float(CAP * j)), 1.0, 0.0).T.astype(BF16)
        second.append(dot(pick, got[...]))
        first.append(by_t(first_pick, own_slab[j]))
    slab = [classes[c][:, 0:samples] for c in range(2)]
    values = []
    for c in range(2):
        for i in range(2):
            mine = first[i] * slab[c]
            for j in range(2):
                values.append(jnp.sum(mine * second[j], axis=1, keepdims=True))
    for side in (first, second):
        for c in range(2):
            for i in range(2):
                values.append(jnp.sum(side[i] * slab[c], axis=1, keepdims=True))
    values += [jnp.broadcast_to(counts[c][:, 0:1], (pairs, 1)) for c in range(2)]
    lane = iota((pairs, block), 1)
    refit = jnp.zeros((pairs, block), F32)
    for v, value in enumerate(values):
        refit = jnp.where(lane == v, value, refit)
    refit = fixed(refit, 2 * samples)
    for out in outs:
        out[block + 8:, :] = refit


def complete(cells, margin_a, margin_b, totals):
    table = [[[None] * 3 for _ in range(3)] for _ in range(2)]
    for c in range(2):
        n = table[c]
        for i in range(2):
            for j in range(2):
                n[i][j] = cells[c][i][j]
            n[i][2] = margin_a[c][i] - n[i][0] - n[i][1]
        for j in range(2):
            n[2][j] = margin_b[c][j] - n[0][j] - n[1][j]
        n[2][2] = (totals[c] - margin_a[c][0] - margin_a[c][1]) - n[2][0] - n[2][1]
    return table


def kirkwood(n, margin_a, margin_b, totals):
    row_ic = [[margin_a[c][0], margin_a[c][1], totals[c] - margin_a[c][0] - margin_a[c][1]] for c in range(2)]
    col_jc = [[margin_b[c][0], margin_b[c][1], totals[c] - margin_b[c][0] - margin_b[c][1]] for c in range(2)]
    single_a = [row_ic[0][i] + row_ic[1][i] for i in range(3)]
    single_b = [col_jc[0][j] + col_jc[1][j] for j in range(3)]
    grand = totals[0] + totals[1]
    inv_a = [1.0 / s for s in single_a]
    row_x = [[row_ic[c][i] * inv_a[i] / totals[c] for i in range(3)] for c in range(2)]
    col_y = [[col_jc[c][j] / single_b[j] for j in range(3)] for c in range(2)]
    scale = None
    approx = {}
    for i in range(3):
        for j in range(3):
            pair = n[0][i][j] + n[1][i][j]
            for c in range(2):
                value = pair * row_x[c][i] * col_y[c][j]
                approx[c, i, j] = value
                scale = value if scale is None else scale + value
    factor = scale / grand
    total = None
    for (c, i, j), value in approx.items():
        term = n[c][i][j] * jnp.log(n[c][i][j] * factor / value)
        total = term if total is None else total + term
    return 2.0 * total


def finish_kernel(b0, b1, b2, b3, a0, a1, a2, a3, screen, stat, columns, *, samples):
    k = lax.axis_index("samp")
    bs, as_ = (b0, b1, b2, b3), (a0, a1, a2, a3)
    block = b0.shape[1]
    quarter = block // 4
    pairs = stat.shape[1]

    def value(m, row):
        return floating(m[row:row + 1, :], 2 * samples)

    def count(m, c):
        if m.shape[0] == block + 8:
            return value(m, block + 4 + c)
        return jnp.broadcast_to(floating(m[block + 8:block + 9, 16 + c:17 + c], 2 * samples), (1, block))

    totals_row = [count(b0, c) + count(b2, c) for c in range(2)]
    own = [value(b0, block + 4 + v) + value(b2, block + 4 + v) for v in range(4)]
    columns[...] = jnp.concatenate(own + [jnp.zeros((block - 4, block), F32)], axis=0).T
    mine = columns[pl.ds(pl.multiple_of(k * quarter, quarter), quarter), :]
    margin_a = [[jnp.broadcast_to(mine[:, c * 2 + i:c * 2 + i + 1], (quarter, block)) for i in range(2)] for c in range(2)]

    stats = []
    for msgs in (bs, as_):
        for parity in range(2):
            x, y = msgs[parity], msgs[parity + 2]
            steps = [[code_step(count(m, c)) for m in (x, y)] for c in range(2)]
            margin_b = [[value(x, block + c * 2 + j) + value(y, block + c * 2 + j) for j in range(2)] for c in range(2)]
            cells = [[[None, None], [None, None]] for _ in range(2)]
            for i in range(2):
                for j in range(2):
                    start = (j * 2 + i) * quarter
                    words = [m[start:start + quarter, :] for m in (x, y)]
                    for c in range(2):
                        codes = [lax.shift_right_arithmetic(w if c == 0 else lax.shift_left(w, 16), 16) for w in words]
                        base = MIDDLE * (margin_a[c][i] + margin_b[c][j]) - (MIDDLE * MIDDLE) * totals_row[c]
                        cells[c][i][j] = (codes[0].astype(F32) * steps[c][0] + codes[1].astype(F32) * steps[c][1]) + base
            table = complete(cells, margin_a, margin_b, totals_row)
            stats.append(kirkwood(table, margin_a, margin_b, totals_row))
    even = (k & 1) == 0
    for side in range(2):
        e, o = stats[2 * side], stats[2 * side + 1]
        screen[:, 2 * side, :] = jnp.where(even, e, o)
        screen[:, 2 * side + 1, :] = jnp.where(even, o, e)

    for start in range(0, pairs, block):
        take = min(block, pairs - start)
        rows = slice(block + 8 + start, block + 8 + start + take)
        sums = floating(b0[rows, 0:block] + b1[rows, 0:block] + b2[rows, 0:block] + b3[rows, 0:block], 2 * samples)
        if take < block:
            sums = jnp.concatenate([sums, jnp.ones((block - take, block), F32)], axis=0)
        turned = sums.T
        row = [turned[v:v + 1, :] for v in range(16)]
        cells = [[[row[c * 4 + i * 2 + j] for j in range(2)] for i in range(2)] for c in range(2)]
        ma = [[row[8 + c * 2 + i] for i in range(2)] for c in range(2)]
        mb = [[row[12 + c * 2 + j] for j in range(2)] for c in range(2)]
        n = complete(cells, ma, mb, totals_row)
        n_ij = [[n[0][i][j] + n[1][i][j] for j in range(3)] for i in range(3)]
        n_ic = [[n[c][i][0] + n[c][i][1] + n[c][i][2] for i in range(3)] for c in range(2)]
        n_jc = [[n[c][0][j] + n[c][1][j] + n[c][2][j] for j in range(3)] for c in range(2)]

        def sweep(_, flat):
            f = [[[flat[c * 9 + i * 3 + j] for j in range(3)] for i in range(3)] for c in range(2)]
            for i in range(3):
                for j in range(3):
                    ratio = n_ij[i][j] / (f[0][i][j] + f[1][i][j])
                    for c in range(2):
                        f[c][i][j] = f[c][i][j] * ratio
            for c in range(2):
                for i in range(3):
                    ratio = n_ic[c][i] / (f[c][i][0] + f[c][i][1] + f[c][i][2])
                    for j in range(3):
                        f[c][i][j] = f[c][i][j] * ratio
                for j in range(3):
                    ratio = n_jc[c][j] / (f[c][0][j] + f[c][1][j] + f[c][2][j])
                    for i in range(3):
                        f[c][i][j] = f[c][i][j] * ratio
            return tuple(f[c][i][j] for c in range(2) for i in range(3) for j in range(3))

        fitted = lax.fori_loop(0, ITERS, sweep, tuple(jnp.ones((1, block), F32) for _ in range(18)))
        total = None
        for c in range(2):
            for i in range(3):
                for j in range(3):
                    term = n[c][i][j] * jnp.log(n[c][i][j] / fitted[c * 9 + i * 3 + j])
                    total = term if total is None else total + term
        stat[:, start:start + take] = (2.0 * total)[:, 0:take]


def vmem(count):
    return [pl.BlockSpec(memory_space=pltpu.VMEM)] * count


def run(body, args, outs, scratch, near=True):
    return pl.pallas_call(
        body,
        out_shape=[pltpu.VMEM(o.shape, o.dtype) if near else o for o in outs],
        in_specs=vmem(len(args)),
        out_specs=vmem(len(outs)),
        scratch_shapes=scratch,
    )(*(pltpu.with_memory_space_constraint(a, pltpu.VMEM) for a in args))


def stage_kernel(geno, label0, own_ids, peer_ids, out, label_copy, own_copy, peer_copy, placed, sems):
    rows, block = geno.shape
    copies = [
        pltpu.make_async_copy(src, dst, sems.at[n])
        for n, (src, dst) in enumerate(((geno, out.at[0:rows]), (label0, label_copy), (own_ids, own_copy), (peer_ids, peer_copy)))
    ]
    for copy in copies:
        copy.start()
    for copy in copies[1:]:
        copy.wait()
    placed[...] = jnp.where(iota(placed.shape, 0) == lax.axis_index("snp"), peer_copy[...], 0)
    case = label_copy[...].astype(F32)
    parts = [case[:, q * block:(q + 1) * block] for q in range(case.shape[1] // block)]
    parts.append(jnp.zeros((out.shape[0] - rows - len(parts), block), F32))
    out[rows:, :] = jnp.concatenate(parts, axis=0).astype(BF16)
    copies[0].wait()


def on_device(genotypes, case_labels, refit_own, refit_peer):
    samples, _, block = genotypes.shape
    pairs = refit_peer.shape[0]
    snp_count = lax.axis_size("snp")
    samp_count = lax.axis_size("samp")
    assert samp_count == 2 * HALF and block & (block - 1) == 0
    shift = block.bit_length() - 1

    def moved(value, where):
        links = []
        for b in range(snp_count):
            for k in range(samp_count):
                to_b, to_k = where(b, k)
                links.append((b * samp_count + k, (to_b % snp_count) * samp_count + to_k % samp_count))
        return lax.ppermute(value, ("snp", "samp"), links)

    geno = genotypes.reshape(2 * samples, block)
    labels = case_labels.reshape(1, samples)
    row_of = lambda count: pltpu.VMEM((1, count), jnp.int32)
    height = 2 * samples + samples // block + -(samples // block) % 8
    stage = pl.pallas_call(
        stage_kernel,
        out_shape=[pltpu.VMEM((height, block), BF16), row_of(samples), row_of(pairs), row_of(pairs),
                   pltpu.VMEM((snp_count, pairs), jnp.int32)],
        in_specs=[pl.BlockSpec(memory_space=pl.ANY)] * 4,
        out_specs=vmem(5),
        scratch_shapes=[pltpu.SemaphoreType.DMA((4,))],
    )
    marked, labels, own_ids, peer_ids, placed = stage(geno, labels, refit_own[None, :], refit_peer[None, :])
    other0 = moved(geno, lambda b, k: (b + 1 + (k & 1), k))
    other1 = moved(geno, lambda b, k: (b + 2 - (k & 1), k ^ 1))
    own1 = moved(marked, lambda b, k: (b, k ^ 1))
    ids = lax.psum(placed, "snp")
    wide = pltpu.VMEM((2 * samples, block), F32)
    (sent,) = run(
        functools.partial(select_kernel, shift=shift), (ids, marked),
        [jax.ShapeDtypeStruct((snp_count * 2 * CAP, samples), BF16)], [wide],
    )
    got = lax.all_to_all(sent, "snp", split_axis=0, concat_axis=0, tiled=True)
    scratch = [wide, pltpu.VMEM((4, 4, block // 4, 2 * samples), BF16), pltpu.VMEM((2 * samples, 2 * block), BF16)]
    short = jax.ShapeDtypeStruct((block + 8, block), jnp.int32)
    tall = jax.ShapeDtypeStruct((block + 8 + pairs, block), jnp.int32)
    *ahead, sums = run(
        ahead_kernel, (marked, own1, other0, other1, labels),
        [short] * 4 + [jax.ShapeDtypeStruct((8, 2 * block), F32)], scratch,
    )
    for d in range(4):
        ahead[d] = moved(ahead[d], lambda b, k: (b - 1 - (k & 1), k ^ d))
    behind = run(
        functools.partial(behind_kernel, shift=shift),
        (marked, own1, other0, other1, labels, own_ids, peer_ids, got, sums),
        [tall] * 4, scratch,
    )
    behind = list(behind)
    for d in range(1, 4):
        behind[d] = moved(behind[d], lambda b, k: (b, k ^ d))
    screen, stat = run(
        functools.partial(finish_kernel, samples=samples), (*behind, *ahead),
        [jax.ShapeDtypeStruct((block // samp_count, 2 * HALF, block), F32), jax.ShapeDtypeStruct((1, pairs), F32)],
        [pltpu.VMEM((block, block), F32)], near=False,
    )
    return screen, stat.reshape(pairs)


def solution(mesh):
    in_specs = (P("samp", None, "snp"), P("samp"), P("snp"), P("snp"))
    out_specs = (P(("snp", "samp"), None, None), P("snp"))

    return jax.shard_map(on_device, mesh=mesh, in_specs=in_specs, out_specs=out_specs, check_vma=False)
```

```python
import functools

import jax
import jax.numpy as jnp
from jax import lax
from jax.experimental import pallas as pl
from jax.experimental.pallas import tpu as pltpu
from jax.sharding import PartitionSpec as P

HALF = 2
CAP = 4
ITERS = 10
MIDDLE = 0.47
GRANT = 24 << 20
SPREAD = 0.411
F32 = jnp.float32
BF16 = jnp.bfloat16


def iota(shape, axis):
    return lax.broadcasted_iota(jnp.int32, shape, axis)


def by_t(a, b):
    return lax.dot_general(a, b, (((1,), (1,)), ((), ())), preferred_element_type=F32)


def dot(a, b):
    return lax.dot_general(a, b, (((1,), (0,)), ((), ())), preferred_element_type=F32)


def earlier(count):
    return (iota((count, count), 0) < iota((count, count), 1)).astype(BF16)


def split_genotypes(ref, wide):
    rows = wide.shape[0]
    wide[...] = ref[0:rows, :].astype(F32)
    return [wide[pl.ds(j, rows // 2, stride=2), :] for j in range(2)]


def select_kernel(ids, geno, sent, wide, *, shift):
    here = lax.axis_index("snp")
    blocks, pairs = ids.shape
    block = geno.shape[1]
    rows = blocks * 2 * CAP
    names = ids[...]
    local = (names & (block - 1)).astype(F32)
    hit = (lax.shift_right_logical(names, shift) == here).astype(F32)
    rank = dot(hit.astype(BF16), earlier(pairs))
    spread = (lax.shift_right_logical(iota((rows, blocks), 0), 3) == iota((rows, blocks), 1)).astype(BF16)
    hit_rows = dot(spread, hit.astype(BF16))
    rank_rows = dot(spread, rank.astype(BF16))
    local_rows = dot(spread, local.astype(BF16))
    slot = (iota((rows, pairs), 0) & (CAP - 1)).astype(F32)
    chosen = jnp.where(rank_rows == slot, hit_rows, 0.0)
    column = jnp.sum(chosen * local_rows, axis=1, keepdims=True)
    valid = jnp.sum(chosen, axis=1, keepdims=True)
    which = iota((rows, block), 1).astype(F32)
    second = (iota((rows, block), 0) & CAP) > 0
    one_hot = jnp.where((which == column) & (valid > 0.5), 1.0, 0.0)
    low = jnp.where(second, 0.0, one_hot).astype(BF16)
    high = jnp.where(second, one_hot, 0.0).astype(BF16)
    g0, g1 = split_genotypes(geno, wide)
    sent[...] = (by_t(low, g0.astype(BF16)) + by_t(high, g1.astype(BF16))).astype(BF16)


def fixed(value, samples):
    return (value * 2.0 ** (30 - (samples - 1).bit_length())).astype(jnp.int32)


def floating(value, samples):
    return value.astype(F32) * 2.0 ** ((samples - 1).bit_length() - 30)


def code_step(count):
    return jnp.maximum(count, 1.0) * (SPREAD * SPREAD / 32767.0)


def quantized(value, step):
    scaled = value * (1.0 / step)
    return jnp.clip(jnp.floor(scaled + 0.5), -32767.0, 32767.0).astype(jnp.int32)


def class_rows(label0, tail):
    case0 = label0[...].astype(F32)
    case1 = jnp.concatenate([tail[q:q + 1, :].astype(F32) for q in range(case0.shape[1] // tail.shape[1])], axis=1)
    case = jnp.concatenate([case0, case1], axis=1)
    return [case, 1.0 - case]


def turn(parts, classes, half, left):
    k = lax.axis_index("samp")
    samples, block = parts[0].shape
    quarter = block // 4
    for i in range(2):
        turned = parts[i].T
        for c in range(2):
            piece = (turned * classes[c][:, half * samples:(half + 1) * samples]).astype(BF16)
            for q in range(4):
                left[q ^ k, c * 2 + i] = piece[q * quarter:(q + 1) * quarter]


def lay(parts, right):
    block = parts[0].shape[1]
    for j in range(2):
        right[:, j * block:(j + 1) * block] = parts[j].astype(BF16)


def prepare_kernel(own0, own1, other1, label0,
                   own_left0, own_left1, own_right0, own_right1, other_left1, other_right1, wide):
    classes = class_rows(label0, own1[wide.shape[0]:, :])
    for ref, half, left, right in ((own0, 0, own_left0, own_right0), (own1, 1, own_left1, own_right1),
                                   (other1, 1, other_left1, other_right1)):
        parts = split_genotypes(ref, wide)
        turn(parts, classes, half, left)
        lay(parts, right)


def coded_tiles(lefts, rights, classes, outs):
    samples = rights[0].shape[0]
    block = rights[0].shape[1] // 2
    quarter = block // 4
    lhs = [left[...].reshape(16 * quarter, samples) for left in lefts]
    cells = dot(lhs[0], rights[0][...]) + dot(lhs[1], rights[1][...])
    ones = jnp.ones((samples, block), BF16)
    row_sums = dot(lhs[0], ones) + dot(lhs[1], ones)
    weights = jnp.concatenate(classes + [jnp.zeros((6, 2 * samples), F32)], axis=0).astype(BF16)
    column_sums = dot(weights[:, 0:samples], rights[0][...]) + dot(weights[:, samples:], rights[1][...])
    lanes = jnp.ones((1, 2 * block), F32)
    counts = [jnp.sum(classes[c], axis=1, keepdims=True) * lanes for c in range(2)]
    for d in range(4):
        words = None
        for c in range(2):
            rows = slice((d * 2 + c) * 2 * quarter, (d * 2 + c + 1) * 2 * quarter)
            row = row_sums[rows]
            base = jnp.concatenate([row, row], axis=1)
            centred = cells[rows] - MIDDLE * (base + column_sums[c:c + 1]) + (MIDDLE * MIDDLE) * counts[c]
            code = quantized(centred, code_step(counts[c]))
            words = lax.shift_left(code, 16) if c == 0 else words | (code & 0xFFFF)
        for j in range(2):
            outs[d][j * 2 * quarter:(j + 1) * 2 * quarter, :] = words[:, j * block:(j + 1) * block]
    return column_sums, counts


def write_tails(outs, samples, block, groups):
    rows = []
    for group in groups:
        for row in group:
            rows += [row[:, j:j + block] for j in range(0, row.shape[1], block)]
    rows.append(jnp.zeros((8 - len(rows), block), F32))
    tail = fixed(jnp.concatenate(rows[:-1] if len(rows) == 9 else rows, axis=0), 2 * samples)
    for out in outs:
        out[block:block + 8, :] = tail


def ahead_kernel(other0, own1, own_right0, own_right1, other_left1, label0,
                 a0, a1, a2, a3, sums, other_right0, wide, other_left0):
    samples = wide.shape[0] // 2
    block = wide.shape[1]
    classes = class_rows(label0, own1[2 * samples:, :])
    outs = (a0, a1, a2, a3)
    parts = split_genotypes(other0, wide)
    turn(parts, classes, 0, other_left0)
    lay(parts, other_right0)
    columns, counts = coded_tiles((other_left0, other_left1), (own_right0, own_right1), classes, outs)
    write_tails(outs, samples, block, ((columns[0:1], columns[1:2]), (counts[0][:, 0:block], counts[1][:, 0:block])))
    sums[...] = columns


def behind_kernel(own1, own_left0, own_left1, own_right0, other_right0, other_right1, label0, own_ids, peer_ids, got, sums,
                  b0, b1, b2, b3, *, shift):
    samples = own_right0.shape[0]
    block = own_right0.shape[1] // 2
    classes = class_rows(label0, own1[2 * samples:, :])
    outs = (b0, b1, b2, b3)
    columns, counts = coded_tiles((own_left0, own_left1), (other_right0, other_right1), classes, outs)
    own_slab = [own_right0[:, j * block:(j + 1) * block] for j in range(2)]
    write_tails(outs, samples, block, ((columns[0:1], columns[1:2]), (sums[0:1, :], sums[1:2, :])))

    pairs = peer_ids.shape[1]
    rows = got.shape[0]
    blocks = rows // (2 * CAP)
    peers = lax.shift_right_logical(peer_ids[...], shift)
    member = (iota((blocks, pairs), 0) == peers).astype(F32)
    before = dot(member.astype(BF16), earlier(pairs))
    rank = jnp.sum(member * before, axis=0, keepdims=True)
    row = iota((rows, pairs), 0)
    row_block = lax.shift_right_logical(row, 3)
    row_slot = (row & (2 * CAP - 1)).astype(F32)
    first_pick = (iota((block, pairs), 0) == own_ids[...]).astype(F32).T.astype(BF16)
    first, second = [], []
    for j in range(2):
        pick = jnp.where((row_block == peers) & (row_slot == rank + float(CAP * j)), 1.0, 0.0).T.astype(BF16)
        second.append(dot(pick, got[...]))
        first.append(by_t(first_pick, own_slab[j]))
    slab = [classes[c][:, 0:samples] for c in range(2)]
    values = []
    for c in range(2):
        for i in range(2):
            mine = first[i] * slab[c]
            for j in range(2):
                values.append(jnp.sum(mine * second[j], axis=1, keepdims=True))
    for side in (first, second):
        for c in range(2):
            for i in range(2):
                values.append(jnp.sum(side[i] * slab[c], axis=1, keepdims=True))
    values += [jnp.broadcast_to(counts[c][:, 0:1], (pairs, 1)) for c in range(2)]
    lane = iota((pairs, block), 1)
    refit = jnp.zeros((pairs, block), F32)
    for v, value in enumerate(values):
        refit = jnp.where(lane == v, value, refit)
    refit = fixed(refit, 2 * samples)
    for out in outs:
        out[block + 8:, :] = refit


def complete(cells, margin_a, margin_b, totals):
    table = [[[None] * 3 for _ in range(3)] for _ in range(2)]
    for c in range(2):
        n = table[c]
        for i in range(2):
            for j in range(2):
                n[i][j] = cells[c][i][j]
            n[i][2] = margin_a[c][i] - n[i][0] - n[i][1]
        for j in range(2):
            n[2][j] = margin_b[c][j] - n[0][j] - n[1][j]
        n[2][2] = (totals[c] - margin_a[c][0] - margin_a[c][1]) - n[2][0] - n[2][1]
    return table


def row_terms(margin_a, totals):
    row_ic = [[margin_a[c][0], margin_a[c][1], totals[c] - margin_a[c][0] - margin_a[c][1]] for c in range(2)]
    single = [row_ic[0][i] + row_ic[1][i] for i in range(3)]
    share = [[row_ic[c][i] / (single[i] * totals[c]) for i in range(3)] for c in range(2)]
    inverse = [[single[i] * totals[c] / row_ic[c][i] for i in range(3)] for c in range(2)]
    return share, inverse


def kirkwood(n, rows, margin_b, totals):
    share, inverse = rows
    col_jc = [[margin_b[c][0], margin_b[c][1], totals[c] - margin_b[c][0] - margin_b[c][1]] for c in range(2)]
    single_b = [col_jc[0][j] + col_jc[1][j] for j in range(3)]
    col_y = [[col_jc[c][j] / single_b[j] for j in range(3)] for c in range(2)]
    col_z = [[single_b[j] / col_jc[c][j] for j in range(3)] for c in range(2)]
    grand = totals[0] + totals[1]
    scale = None
    ratio = {}
    for i in range(3):
        for j in range(3):
            pair = n[0][i][j] + n[1][i][j]
            inv_pair = 1.0 / pair
            for c in range(2):
                value = pair * share[c][i] * col_y[c][j]
                ratio[c, i, j] = n[c][i][j] * (inv_pair * inverse[c][i] * col_z[c][j])
                scale = value if scale is None else scale + value
    factor = scale / grand
    total = None
    for (c, i, j), value in ratio.items():
        term = n[c][i][j] * jnp.log(value * factor)
        total = term if total is None else total + term
    return 2.0 * total


def finish_kernel(b0, b1, b2, b3, a0, a1, a2, a3, screen, stat, columns, *, samples):
    k = lax.axis_index("samp")
    bs, as_ = (b0, b1, b2, b3), (a0, a1, a2, a3)
    block = b0.shape[1]
    quarter = block // 4
    pairs = stat.shape[1]

    def value(m, row):
        return floating(m[row:row + 1, :], 2 * samples)

    def count(m, c):
        if m.shape[0] == block + 8:
            return value(m, block + 4 + c)
        return jnp.broadcast_to(floating(m[block + 8:block + 9, 16 + c:17 + c], 2 * samples), (1, block))

    totals_row = [count(b0, c) + count(b2, c) for c in range(2)]
    own = [value(b0, block + 4 + v) + value(b2, block + 4 + v) for v in range(4)]
    columns[...] = jnp.concatenate(own + [jnp.zeros((block - 4, block), F32)], axis=0).T
    mine = columns[pl.ds(pl.multiple_of(k * quarter, quarter), quarter), :]
    margin_a = [[jnp.broadcast_to(mine[:, c * 2 + i:c * 2 + i + 1], (quarter, block)) for i in range(2)] for c in range(2)]

    rows_of = row_terms(margin_a, totals_row)
    stats = []
    for msgs in (bs, as_):
        for parity in range(2):
            x, y = msgs[parity], msgs[parity + 2]
            steps = [[code_step(count(m, c)) for m in (x, y)] for c in range(2)]
            margin_b = [[value(x, block + c * 2 + j) + value(y, block + c * 2 + j) for j in range(2)] for c in range(2)]
            cells = [[[None, None], [None, None]] for _ in range(2)]
            for i in range(2):
                for j in range(2):
                    start = (j * 2 + i) * quarter
                    words = [m[start:start + quarter, :] for m in (x, y)]
                    for c in range(2):
                        codes = [lax.shift_right_arithmetic(w if c == 0 else lax.shift_left(w, 16), 16) for w in words]
                        base = MIDDLE * (margin_a[c][i] + margin_b[c][j]) - (MIDDLE * MIDDLE) * totals_row[c]
                        cells[c][i][j] = (codes[0].astype(F32) * steps[c][0] + codes[1].astype(F32) * steps[c][1]) + base
            table = complete(cells, margin_a, margin_b, totals_row)
            stats.append(kirkwood(table, rows_of, margin_b, totals_row))
    even = (k & 1) == 0
    for side in range(2):
        e, o = stats[2 * side], stats[2 * side + 1]
        screen[:, 2 * side, :] = jnp.where(even, e, o)
        screen[:, 2 * side + 1, :] = jnp.where(even, o, e)

    for start in range(0, pairs, block):
        take = min(block, pairs - start)
        rows = slice(block + 8 + start, block + 8 + start + take)
        sums = floating(b0[rows, 0:block] + b1[rows, 0:block] + b2[rows, 0:block] + b3[rows, 0:block], 2 * samples)
        if take < block:
            sums = jnp.concatenate([sums, jnp.ones((block - take, block), F32)], axis=0)
        turned = sums.T
        row = [turned[v:v + 1, :] for v in range(16)]
        cells = [[[row[c * 4 + i * 2 + j] for j in range(2)] for i in range(2)] for c in range(2)]
        ma = [[row[8 + c * 2 + i] for i in range(2)] for c in range(2)]
        mb = [[row[12 + c * 2 + j] for j in range(2)] for c in range(2)]
        n = complete(cells, ma, mb, totals_row)
        n_ij = [[n[0][i][j] + n[1][i][j] for j in range(3)] for i in range(3)]
        n_ic = [[n[c][i][0] + n[c][i][1] + n[c][i][2] for i in range(3)] for c in range(2)]
        n_jc = [[n[c][0][j] + n[c][1][j] + n[c][2][j] for j in range(3)] for c in range(2)]

        def sweep(_, flat):
            f = [[[flat[c * 9 + i * 3 + j] for j in range(3)] for i in range(3)] for c in range(2)]
            for i in range(3):
                for j in range(3):
                    ratio = n_ij[i][j] / (f[0][i][j] + f[1][i][j])
                    for c in range(2):
                        f[c][i][j] = f[c][i][j] * ratio
            for c in range(2):
                for i in range(3):
                    ratio = n_ic[c][i] / (f[c][i][0] + f[c][i][1] + f[c][i][2])
                    for j in range(3):
                        f[c][i][j] = f[c][i][j] * ratio
                for j in range(3):
                    ratio = n_jc[c][j] / (f[c][0][j] + f[c][1][j] + f[c][2][j])
                    for i in range(3):
                        f[c][i][j] = f[c][i][j] * ratio
            return tuple(f[c][i][j] for c in range(2) for i in range(3) for j in range(3))

        fitted = lax.fori_loop(0, ITERS, sweep, tuple(jnp.ones((1, block), F32) for _ in range(18)))
        total = None
        for c in range(2):
            for i in range(3):
                for j in range(3):
                    term = n[c][i][j] * jnp.log(n[c][i][j] / fitted[c * 9 + i * 3 + j])
                    total = term if total is None else total + term
        stat[:, start:start + take] = (2.0 * total)[:, 0:take]


def vmem(count):
    return [pl.BlockSpec(memory_space=pltpu.VMEM)] * count


def run(body, args, outs, scratch, near=True):
    return pl.pallas_call(
        body,
        out_shape=[pltpu.VMEM(o.shape, o.dtype) if near else o for o in outs],
        in_specs=vmem(len(args)),
        out_specs=vmem(len(outs)),
        scratch_shapes=scratch,
        compiler_params=pltpu.CompilerParams(vmem_limit_bytes=GRANT),
    )(*(pltpu.with_memory_space_constraint(a, pltpu.VMEM) for a in args))


def stage_kernel(geno, label0, own_ids, peer_ids, out, label_copy, own_copy, peer_copy, placed, sems):
    rows, block = geno.shape
    copies = [
        pltpu.make_async_copy(src, dst, sems.at[n])
        for n, (src, dst) in enumerate(((geno, out.at[0:rows]), (label0, label_copy), (own_ids, own_copy), (peer_ids, peer_copy)))
    ]
    for copy in copies:
        copy.start()
    for copy in copies[1:]:
        copy.wait()
    placed[...] = jnp.where(iota(placed.shape, 0) == lax.axis_index("snp"), peer_copy[...], 0)
    case = label_copy[...].astype(F32)
    parts = [case[:, q * block:(q + 1) * block] for q in range(case.shape[1] // block)]
    parts.append(jnp.zeros((out.shape[0] - rows - len(parts), block), F32))
    out[rows:, :] = jnp.concatenate(parts, axis=0).astype(BF16)
    copies[0].wait()


def on_device(genotypes, case_labels, refit_own, refit_peer):
    samples, _, block = genotypes.shape
    pairs = refit_peer.shape[0]
    snp_count = lax.axis_size("snp")
    samp_count = lax.axis_size("samp")
    assert samp_count == 2 * HALF and block & (block - 1) == 0
    shift = block.bit_length() - 1

    def moved(value, where):
        links = []
        for b in range(snp_count):
            for k in range(samp_count):
                to_b, to_k = where(b, k)
                links.append((b * samp_count + k, (to_b % snp_count) * samp_count + to_k % samp_count))
        return lax.ppermute(value, ("snp", "samp"), links)

    geno = genotypes.reshape(2 * samples, block)
    labels = case_labels.reshape(1, samples)
    row_of = lambda count: pltpu.VMEM((1, count), jnp.int32)
    height = 2 * samples + samples // block + -(samples // block) % 8
    stage = pl.pallas_call(
        stage_kernel,
        out_shape=[pltpu.VMEM((height, block), BF16), row_of(samples), row_of(pairs), row_of(pairs),
                   pltpu.VMEM((snp_count, pairs), jnp.int32)],
        in_specs=[pl.BlockSpec(memory_space=pl.ANY)] * 4,
        out_specs=vmem(5),
        scratch_shapes=[pltpu.SemaphoreType.DMA((4,))],
    )
    marked, labels, own_ids, peer_ids, placed = stage(geno, labels, refit_own[None, :], refit_peer[None, :])
    other0 = moved(geno, lambda b, k: (b + 1 + (k & 1), k))
    other1 = moved(geno, lambda b, k: (b + 2 - (k & 1), k ^ 1))
    own1 = moved(marked, lambda b, k: (b, k ^ 1))
    ids = lax.psum(placed, "snp")
    wide = pltpu.VMEM((2 * samples, block), F32)
    (sent,) = run(
        functools.partial(select_kernel, shift=shift), (ids, marked),
        [jax.ShapeDtypeStruct((snp_count * 2 * CAP, samples), BF16)], [wide],
    )
    got = lax.all_to_all(sent, "snp", split_axis=0, concat_axis=0, tiled=True)
    left = jax.ShapeDtypeStruct((4, 4, block // 4, samples), BF16)
    right = jax.ShapeDtypeStruct((samples, 2 * block), BF16)
    own_left0, own_left1, own_right0, own_right1, other_left1, other_right1 = run(
        prepare_kernel, (marked, own1, other1, labels), [left, left, right, right, left, right], [wide])
    short = jax.ShapeDtypeStruct((block + 8, block), jnp.int32)
    tall = jax.ShapeDtypeStruct((block + 8 + pairs, block), jnp.int32)
    *ahead, sums, other_right0 = run(
        ahead_kernel, (other0, own1, own_right0, own_right1, other_left1, labels),
        [short] * 4 + [jax.ShapeDtypeStruct((8, 2 * block), F32), right], [wide, pltpu.VMEM(left.shape, BF16)],
    )
    for d in range(4):
        ahead[d] = moved(ahead[d], lambda b, k: (b - 1 - (k & 1), k ^ d))
    behind = run(
        functools.partial(behind_kernel, shift=shift),
        (own1, own_left0, own_left1, own_right0, other_right0, other_right1, labels, own_ids, peer_ids, got, sums),
        [tall] * 4, [],
    )
    behind = list(behind)
    for d in range(1, 4):
        behind[d] = moved(behind[d], lambda b, k: (b, k ^ d))
    screen, stat = run(
        functools.partial(finish_kernel, samples=samples), (*behind, *ahead),
        [jax.ShapeDtypeStruct((block // samp_count, 2 * HALF, block), F32), jax.ShapeDtypeStruct((1, pairs), F32)],
        [pltpu.VMEM((block, block), F32)], near=False,
    )
    return screen, stat.reshape(pairs)


def solution(mesh):
    in_specs = (P("samp", None, "snp"), P("samp"), P("snp"), P("snp"))
    out_specs = (P(("snp", "samp"), None, None), P("snp"))

    return jax.shard_map(on_device, mesh=mesh, in_specs=in_specs, out_specs=out_specs, check_vma=False)
```
